768 devices in a mesh: blk: 48 (over y, z_hi, core), col: 16 (over z_lo, x).
Axes of the slice: x: 4, y: 8, z: 12 (z_hi: 3, z_lo: 4; z = z_hi * 4 + z_lo), core: 2. Of those that a mesh axis runs over, the one named last changes fastest.
Arguments:
- features: bfloat16 [512, 196608], P('col', 'blk'), may hold values from -6 to 6
- band_weights: bfloat16 [196608, 384], P('blk'), may hold values from -0.3125 to 0.3125
- hub_ids: int32 [3072], P('blk'), may hold values from 0 to 196607, as said below
- tile_rows: int32 [6144], P('blk'), may hold values from 0 to 1535, as said below
- tile_cols: int32 [6144], P('blk'), may hold values from 0 to 23
- tile_vals: bfloat16 [6144, 128, 128], P('blk'), may hold values from -0.3125 to 0.3125
- tile_counts: int32 [48], P('blk'), may hold values from 1 to 128, as said below
- weight: bfloat16 [512, 512], replicated, may hold values from -0.25 to 0.25
- cotangent: bfloat16 [512, 196608], P('col', 'blk'), may hold values from -0.013671875 to 0.013671875
Outputs:
- activation: bfloat16 [512, 196608], P('col', 'blk')
- weight_grad: float32 [512, 512], P('col')
The draws below stay inside these ranges and needn't reach their ends.
Inputs may be any that keep to these rules, and one draw needn't show every extreme that they name: `hub_ids`: each partition lists 64 distinct passages of its own rows, its first and its last passage among them. `tile_rows`: every slot of partition p names a row block of partition p's own passages; its slot 0 names the partition's first row block and its slot 1 its last. Partition p uses its first tile_counts[p] slots; some partition uses all 128.
All inputs are finite; a program needn't handle non-finite values.
Results may differ from the reference program's by a relative error of at most 0.0056.
Values may be sent and summed in bfloat16 or wider, within the bound.
A program may use at most 32 MiB of HBM per device.

```python
import jax
import jax.numpy as jnp
from jax import lax

F = 512
H = 512
TILE = 128
ROWS_DEV = 4096
HUB_DEV = 64
HCAP = 128
PASSAGES = 196608
HUBS = 3072
SLOTS = 6144
N_BLK = 48


def draw_hub_ids(key, part):
    keys = jax.random.split(key, N_BLK)

    def pick_one(one_key):
        first_key, second_key = jax.random.split(one_key)
        order = jax.random.permutation(first_key, ROWS_DEV - 2) + 1
        chosen = jnp.concatenate([order[:HUB_DEV - 2], jnp.zeros((1,), jnp.int32), jnp.full((1,), ROWS_DEV - 1, jnp.int32)]).astype(jnp.int32)
        return jax.random.permutation(second_key, chosen)
    local_ids = jax.vmap(pick_one)(keys)
    offsets = (jnp.arange(N_BLK, dtype=jnp.int32) * ROWS_DEV)[:, None]
    return (local_ids + offsets).reshape(-1).astype(jnp.int32)


def draw_tile_rows(key, part):
    block_rows = ROWS_DEV // 128
    local_blocks = jax.random.randint(key, (N_BLK, HCAP), 0, block_rows)
    slot_index = jnp.arange(HCAP, dtype=jnp.int32)[None, :]
    local_blocks = jnp.where(slot_index == 0, 0, local_blocks)
    local_blocks = jnp.where(slot_index == 1, block_rows - 1, local_blocks)
    offsets = (jnp.arange(N_BLK, dtype=jnp.int32) * block_rows)[:, None]
    return (local_blocks + offsets).reshape(-1).astype(jnp.int32)


def draw_tile_counts(key, part):
    lower = max(1, HCAP // 5)
    upper = max(lower + 1, HCAP * 5 // 8 + 1)
    counts = jax.random.randint(key, (N_BLK,), lower, upper)
    busiest = jax.random.randint(jax.random.fold_in(key, 7), (), 0, N_BLK)
    return jnp.where(jnp.arange(N_BLK) == busiest, HCAP, counts).astype(jnp.int32)


def plant(result, stream_key, smallest, top_value):
    shape = result.shape
    place = [jax.random.randint(jax.random.fold_in(stream_key, axis), (), 0, shape[axis]) for axis in range(len(shape))]
    result = result.at[tuple(place)].set(smallest)
    longest = shape.index(max(shape))
    place[longest] = (place[longest] + 1) % shape[longest]
    return result.at[tuple(place)].set(top_value)


def steps_of(rng, extent, pieces, least, largest):
    loudness, own = 1.0, jax.random.fold_in(rng, 6)
    for axis_at, parts in pieces:
        steps = jnp.exp(jax.random.uniform(jax.random.fold_in(own, axis_at), (parts,), jnp.float32, least / len(pieces), largest / len(pieces)))
        loudness = loudness * jnp.repeat(steps, extent[axis_at] // parts).reshape([-1 if axis == axis_at else 1 for axis in range(len(extent))])
    return loudness


def centred(key, extent, scale, bound, shards=(), held_as=jnp.bfloat16):
    values = jax.random.normal(key, extent, jnp.float32) * scale
    if len(shards) > 0:
        values = steps_of(key, extent, shards, -0.22, 0.18) * values
    return jnp.clip(values, min=-bound, max=bound).astype(held_as)


def setup_inputs(seed: int = 0) -> dict:
    seeds = jax.random.split(jax.random.key(seed), 10)
    features = centred(seeds[0], (F, PASSAGES), 1.0, 6.0, ((0, 16), (1, 48)))
    band_weights = centred(seeds[1], (PASSAGES, 3 * TILE), (3 * TILE) ** -0.5, 0.3125, ((0, 48),))
    hub_ids = draw_hub_ids(jax.random.fold_in(seeds[9], 71), 0)
    tile_rows = draw_tile_rows(jax.random.fold_in(seeds[9], 71), 0)
    tile_cols = plant(jax.random.randint(seeds[4], (SLOTS,), 0, HUBS // TILE), jax.random.fold_in(seeds[4], 1), 0, (HUBS // TILE) - 1).astype(jnp.int32)
    tile_vals = centred(seeds[5], (SLOTS, TILE, TILE), (3 * TILE) ** -0.5, 0.3125, ((0, 48),))
    tile_counts = draw_tile_counts(jax.random.fold_in(seeds[9], 71), 0)
    weight = centred(seeds[7], (H, F), F ** -0.5, 0.25)
    cotangent = centred(seeds[8], (H, PASSAGES), PASSAGES ** -0.5, 0.013671875, ((0, 16), (1, 48)))
    return dict(features=features, band_weights=band_weights, hub_ids=hub_ids, tile_rows=tile_rows, tile_cols=tile_cols, tile_vals=tile_vals, tile_counts=tile_counts, weight=weight, cotangent=cotangent)


def reference(features, band_weights, hub_ids, tile_rows, tile_cols, tile_vals, tile_counts, weight, cotangent):
    feat_count, passage_count = features.shape
    block_count = passage_count // 128
    blocks = features.reshape(feat_count, block_count, 128).astype(jnp.float32)
    band_blocks = band_weights.reshape(block_count, 128, 3, 128).astype(jnp.float32)
    band_total = jnp.zeros((feat_count, block_count, 128), jnp.float32)
    for offset in range(3):
        shifted = jnp.roll(blocks, 1 - offset, axis=1)
        band_total = band_total + jnp.einsum("fbc,brc->fbr", shifted, band_blocks[:, :, offset, :])
    hub_x = jnp.take(features, hub_ids, axis=1)
    hub_blocks = hub_x.reshape(feat_count, hub_x.shape[1] // 128, 128)
    slot_count = tile_rows.shape[0]
    per_part = slot_count // tile_counts.shape[0]
    slot_index = jnp.arange(slot_count, dtype=jnp.int32)
    in_use = (slot_index % per_part < tile_counts[slot_index // per_part]).astype(jnp.float32)

    def add_tile(carry, item):
        row_block, hub_block, values, use_weight = item
        source = lax.dynamic_index_in_dim(hub_blocks, hub_block, 1, keepdims=False)
        term = jnp.dot(source, values.T, preferred_element_type=jnp.float32) * use_weight
        current = lax.dynamic_index_in_dim(carry, row_block, 1, keepdims=False)
        return lax.dynamic_update_index_in_dim(carry, current + term, row_block, 1), None

    start_total = jnp.zeros((feat_count, block_count, 128), jnp.float32)
    hub_total, ignored = lax.scan(add_tile, start_total, (tile_rows, tile_cols, tile_vals, in_use))
    aggregated = (band_total + hub_total).reshape(feat_count, passage_count).astype(jnp.bfloat16)
    preact = jnp.dot(weight, aggregated, preferred_element_type=jnp.float32)
    activation = jax.nn.silu(preact).astype(jnp.bfloat16)
    sigmoid_pre = jax.nn.sigmoid(preact)
    pre_grad = (cotangent.astype(jnp.float32) * sigmoid_pre * (1.0 + preact * (1.0 - sigmoid_pre))).astype(jnp.bfloat16)
    weight_grad = lax.dot_general(pre_grad, aggregated, (((1,), (1,)), ((), ())), preferred_element_type=jnp.float32)
    return activation, weight_grad
```

```python
import functools

import jax
import jax.numpy as jnp
from jax import lax
from jax.experimental import pallas as pl
from jax.experimental.pallas import tpu as pltpu
from jax.sharding import PartitionSpec as P

MESH = pl.DeviceIdType.MESH
BF = jnp.bfloat16
F32 = jnp.float32
TILE = 128
NY, NZH, NC, NZL, NX = 8, 3, 2, 4, 4
CHIPS = NY * NZH
NZ = NZH * NZL
NYC = NY * NC
NT = (((1,), (1,)), ((), ()))
VMEM = pl.BlockSpec(memory_space=pltpu.VMEM)
ANY = pl.BlockSpec(memory_space=pl.ANY)
SMEM = pl.BlockSpec(memory_space=pltpu.SMEM)


def rcopy(src, dst, send, recv, blk, col):
    return pltpu.make_async_remote_copy(
        src_ref=src,
        dst_ref=dst,
        send_sem=send,
        recv_sem=recv,
        device_id={"blk": blk, "col": col},
        device_id_type=MESH,
    )


def signal(sem, blk, col):
    pl.semaphore_signal(sem, inc=1, device_id={"blk": blk, "col": col}, device_id_type=MESH)


def loop(start, stop, body):
    lax.fori_loop(start, stop, lambda i, c: (body(i), c)[1], 0)


def front_kernel(
    feat, bw, ids, cot, band, hubs, cotg, xe, wv, f_sem, w_sem, h_send, h_recv, s_sem, e_send, e_recv, c_send, c_recv, c_loc
):
    rows = bw.shape[0]
    blocks = rows // TILE
    quarter = rows // NZL
    wchunks = wv.shape[0]
    per = blocks // wchunks
    b = lax.axis_index("blk")
    c = lax.axis_index("col")
    core = lax.rem(b, NC)
    chip = lax.div(b, NC)
    z = lax.div(c, NX)
    x = lax.rem(c, NX)
    sib = b + 1 - 2 * core
    cross = lax.rem(b + 2 * core - 1 + CHIPS * NC, CHIPS * NC)

    f_copy = pltpu.make_async_copy(feat, xe.at[:, pl.ds(TILE, rows)], f_sem)
    f_copy.start()
    w_copies = [
        pltpu.make_async_copy(bw.at[pl.ds(i * per * TILE, per * TILE), :], wv.at[i], w_sem.at[i])
        for i in range(wchunks)
    ]
    for w in w_copies:
        w.start()

    barrier = pltpu.get_barrier_semaphore()

    def peer(d):
        return lax.rem(chip + d, CHIPS) * NC + core

    def zpeer(d):
        return lax.rem(z + d, NZL)

    loop(1, CHIPS, lambda d: signal(barrier, peer(d), c))
    signal(barrier, sib, c)
    signal(barrier, cross, c)
    for d in range(1, NZL):
        signal(barrier, b, zpeer(d) * NX + x)

    f_copy.wait()
    local_ids = ids[...] - b * rows
    lanes = jnp.concatenate([local_ids, local_ids], axis=1)
    step = 256
    picked = jnp.zeros((feat.shape[0], TILE), F32)
    for i in range(rows // step):
        at = lax.broadcasted_iota(jnp.int32, (step, TILE), 0) + i * step
        hot = jnp.where(at == lanes, 1.0, 0.0).astype(BF)
        picked += jnp.dot(xe[:, TILE + i * step : TILE + (i + 1) * step], hot, preferred_element_type=F32)
    half = feat.shape[0] // 2
    low = lax.broadcasted_iota(jnp.int32, (half, TILE), 1) < TILE // 2
    hubs[0, chip] = jnp.where(low, picked[:half], picked[half:]).astype(BF)

    pl.semaphore_wait(barrier, CHIPS - 1 + 2 + NZL - 1)

    def hub_copy(d):
        return rcopy(hubs.at[0, chip], hubs.at[0, chip], h_send.at[d], h_recv.at[d], peer(d), c)

    loop(1, CHIPS, lambda d: hub_copy(d).start())
    end = (blocks - 1) * TILE
    to_sib = rcopy(
        feat.at[:, pl.ds(pl.multiple_of((1 - core) * end, TILE), TILE)],
        xe.at[:, pl.ds(pl.multiple_of(core * (rows + TILE), TILE), TILE)],
        e_send.at[0], e_recv.at[0], sib, c,
    )
    to_cross = rcopy(
        feat.at[:, pl.ds(pl.multiple_of(core * end, TILE), TILE)],
        xe.at[:, pl.ds(pl.multiple_of((1 - core) * (rows + TILE), TILE), TILE)],
        e_send.at[1], e_recv.at[1], cross, c,
    )
    to_cross.start()
    to_sib.start()
    cots = []
    for d in range(1, NZL):
        zz = zpeer(d)
        cots.append(
            rcopy(
                cot.at[:, pl.ds(pl.multiple_of(zz * quarter, TILE), quarter)],
                cotg.at[z], c_send.at[d - 1], c_recv.at[d - 1], b, zz * NX + x,
            )
        )
    for k in cots:
        k.start()
    own_cot = pltpu.make_async_copy(
        cot.at[:, pl.ds(pl.multiple_of(z * quarter, TILE), quarter)], cotg.at[z], c_loc
    )
    own_cot.start()

    def do_band(r):
        i, j = divmod(r, per)
        band[r] = lax.dot_general(
            xe[:, r * TILE : (r + 3) * TILE],
            wv[i, j * TILE : (j + 1) * TILE, :],
            NT,
            preferred_element_type=F32,
        )

    for r in range(blocks):
        if r % per == 0:
            w_copies[r // per].wait()
        if 0 < r < blocks - 1:
            do_band(r)

    loop(1, CHIPS, lambda d: hub_copy(d).wait_recv())
    swap = rcopy(hubs.at[0], hubs.at[1], s_sem.at[0], s_sem.at[1], sib, c)
    swap.start()
    to_cross.wait_recv()
    to_sib.wait_recv()
    do_band(0)
    do_band(blocks - 1)
    swap.wait_recv()
    for k in cots:
        k.wait_recv()
    own_cot.wait()
    loop(1, CHIPS, lambda d: hub_copy(d).wait_send())
    swap.wait_send()
    to_cross.wait_send()
    to_sib.wait_send()
    for k in cots:
        k.wait_send()


def hub_kernel(rows_ref, cols_ref, count_ref, band, hubs, tv, out, tvv, hub, acc, t_sem):
    b = lax.axis_index("blk")
    core = lax.rem(b, NC)
    slots = tv.shape[0]
    blocks = band.shape[0]
    chunks = t_sem.shape[0]
    per = slots // chunks
    copies = [
        pltpu.make_async_copy(tv.at[pl.ds(i * per, per)], tvv.at[pl.ds(i * per, per)], t_sem.at[i])
        for i in range(chunks)
    ]
    for k in copies:
        k.start()
    acc[...] = band[...]
    half = hubs.shape[2]
    mine = hubs[0].astype(F32)
    other = hubs[1].astype(F32)
    first = jnp.where(core == 0, mine, other)
    second = jnp.where(core == 0, other, mine)
    low = lax.broadcasted_iota(jnp.int32, mine.shape, 2) < TILE // 2
    hub[:, :half, :] = jnp.where(low, first, pltpu.roll(second, TILE // 2, 2)).astype(BF)
    hub[:, half:, :] = jnp.where(low, pltpu.roll(first, TILE // 2, 2), second).astype(BF)
    count = count_ref[0]
    base = b * blocks
    for i in range(chunks):
        copies[i].wait()

        @pl.when(i * per < count)
        def _():
            parts = []
            for j in range(per):
                s = i * per + j
                got = lax.dot_general(hub[cols_ref[s]], tvv[s], NT, preferred_element_type=F32)
                parts.append(jnp.where(s < count, got, 0.0))
            for j in range(per):
                r = rows_ref[i * per + j] - base
                acc[r] = acc[r] + parts[j]

    for r in range(blocks):
        out[:, r * TILE : (r + 1) * TILE] = acc[r].astype(BF)


def back_kernel(
    agg, cotg, w3, act_out, wg_out, g, cotv, act, pt, yb, st, zb,
    z_send, z_recv, z_loc, x_send, x_recv, r_send, r_recv, cot_sem,
    a_send, a_recv, a_loc, y_send, y_recv, q_send, q_recv, o_send, o_recv,
):
    rows = agg.shape[1]
    feat_local = agg.shape[0]
    quarter = rows // NZL
    b = lax.axis_index("blk")
    c = lax.axis_index("col")
    core = lax.rem(b, NC)
    y = lax.div(b, NC * NZH)
    zh = lax.rem(lax.div(b, NC), NZH)
    z = lax.div(c, NX)
    x = lax.rem(c, NX)
    right = lax.rem(x + 1, NX)
    left = lax.rem(x + NX - 1, NX)
    me_yc = y * NC + core
    zz_me = zh * NZL + z

    def yc_blk(j):
        return (lax.div(j, NC) * NZH + zh) * NC + lax.rem(j, NC)

    def yc_peer(d):
        return lax.rem(me_yc + d, NYC)

    def z_peer(d):
        at = lax.rem(zz_me + d, NZ)
        return lax.div(at, NZL), lax.rem(at, NZL)

    def z_dev(d):
        h, l = z_peer(d)
        return (y * NZH + h) * NC + core, l * NX + x

    def zl(d):
        return lax.rem(z + d, NZL)

    ccopy = pltpu.make_async_copy(cotg, cotv, cot_sem)
    ccopy.start()
    barrier = pltpu.get_barrier_semaphore()
    for d in range(1, NZL):
        signal(barrier, b, zl(d) * NX + x)
    signal(barrier, b, z * NX + left)
    signal(barrier, b, z * NX + right)
    loop(1, NYC, lambda d: signal(barrier, yc_blk(yc_peer(d)), c))
    loop(1, NZ, lambda d: signal(barrier, *z_dev(d)))
    pl.semaphore_wait(barrier, NZL - 1 + 2 + NYC - 1 + NZ - 1)

    def part(ref, q):
        return ref.at[:, pl.ds(pl.multiple_of(q * quarter, TILE), quarter)]

    zc = [
        rcopy(part(agg, zl(d)), g.at[c], z_send.at[d - 1], z_recv.at[d - 1], b, zl(d) * NX + x)
        for d in range(1, NZL)
    ]
    for k in zc:
        k.start()
    own = pltpu.make_async_copy(part(agg, z), g.at[c], z_loc)
    own.start()

    def x_copy(src_z, src_x, to, send, recv):
        slot = src_z * NX + src_x
        return rcopy(g.at[slot], g.at[slot], send, recv, b, z * NX + to)

    def push(d):
        src = lax.rem(z + NZL - d, NZL)
        x_copy(src, x, right, x_send.at[0, src], x_recv.at[0, src]).start()
        x_copy(src, x, left, x_send.at[1, src], x_recv.at[1, src]).start()

    own.wait()
    push(0)
    for d in range(1, NZL):
        zc[d - 1].wait_recv()
        push(d)
    for s in range(NZL // 2):
        t = s + NZL // 2
        x_copy(s, left, right, x_send.at[0, s], x_recv.at[0, s]).wait_recv()
        x_copy(s, left, right, r_send.at[0, s], r_recv.at[0, s]).start()
        x_copy(t, right, left, x_send.at[1, t], x_recv.at[1, t]).wait_recv()
        x_copy(t, right, left, r_send.at[1, s], r_recv.at[1, s]).start()
    for s in range(NZL // 2):
        t = s + NZL // 2
        x_copy(t, left, right, x_send.at[0, t], x_recv.at[0, t]).wait_recv()
        x_copy(s, right, left, x_send.at[1, s], x_recv.at[1, s]).wait_recv()
    for s in range(NZL // 2):
        x_copy(s, left, right, r_send.at[0, s], r_recv.at[0, s]).wait_recv()
        x_copy(s, left, right, r_send.at[1, s], r_recv.at[1, s]).wait_recv()

    whole = g[...].reshape(NZL * NX * feat_local, quarter)
    ccopy.wait()
    pres = []
    for s in range(NZL):
        pre = jnp.dot(w3[s * NX + x], whole, preferred_element_type=F32)
        sig = jax.nn.sigmoid(pre)
        act[s] = (pre * sig).astype(BF)
        pres.append((cotv[s].astype(F32) * sig * (1.0 + pre * (1.0 - sig))).astype(BF))

    ac = [
        rcopy(act.at[zl(d)], part(act_out, z), a_send.at[d - 1], a_recv.at[d - 1], b, zl(d) * NX + x)
        for d in range(1, NZL)
    ]
    for k in ac:
        k.start()
    own_act = pltpu.make_async_copy(act.at[z], part(act_out, z), a_loc)
    own_act.start()

    for s in range(NZL):
        wg = lax.dot_general(pres[s], whole, NT, preferred_element_type=F32)
        for j in range(NYC):
            rt, lt = divmod(j, 4)
            pt[j, s] = wg[rt * 8 : (rt + 1) * 8, lt * TILE : (lt + 1) * TILE]

    def y_copy(d):
        j = yc_peer(d)
        return rcopy(pt.at[j], yb.at[d], y_send.at[d], y_recv.at[d], yc_blk(j), c)

    loop(1, NYC, lambda d: y_copy(d).start())
    loop(1, NYC, lambda d: y_copy(d).wait_recv())
    total = pt[me_yc]
    for d in range(1, NYC):
        total = total + yb[d]
    st[...] = total

    def q_copy(d):
        return rcopy(st.at[z_peer(d)[1]], zb.at[d], q_send.at[d], q_recv.at[d], *z_dev(d))

    loop(1, NZ, lambda d: q_copy(d).start())
    loop(1, NZ, lambda d: q_copy(d).wait_recv())
    tile = st[z]
    for d in range(1, NZ):
        tile = tile + zb[d]
    wg_out[me_yc] = tile

    def o_copy(d):
        return rcopy(wg_out.at[me_yc], wg_out.at[me_yc], o_send.at[d], o_recv.at[d], yc_blk(yc_peer(d)), c)

    loop(1, NYC, lambda d: o_copy(d).start())
    for k in ac:
        k.wait_recv()
    own_act.wait()
    loop(1, NYC, lambda d: o_copy(d).wait_recv())

    for k in zc:
        k.wait_send()
    for s in range(NZL):
        x_copy(s, x, right, x_send.at[0, s], x_recv.at[0, s]).wait_send()
        x_copy(s, x, left, x_send.at[1, s], x_recv.at[1, s]).wait_send()
    for s in range(NZL // 2):
        x_copy(s, left, right, r_send.at[0, s], r_recv.at[0, s]).wait_send()
        x_copy(s, left, left, r_send.at[1, s], r_recv.at[1, s]).wait_send()
    for k in ac:
        k.wait_send()
    loop(1, NYC, lambda d: y_copy(d).wait_send())
    loop(1, NZ, lambda d: q_copy(d).wait_send())
    loop(1, NYC, lambda d: o_copy(d).wait_send())


DMA = pltpu.SemaphoreType.DMA


def body(
    features, band_weights, hub_ids, tile_rows, tile_cols, tile_vals, tile_counts, weight, cotangent
):
    fl, rows = features.shape
    blocks = rows // TILE
    quarter = rows // NZL
    slots = tile_vals.shape[0]
    cols = NZL * NX
    wchunks = 8
    sds = jax.ShapeDtypeStruct
    band, hubs, cotg = pl.pallas_call(
        front_kernel,
        name="front",
        out_shape=(
            sds((blocks, fl, TILE), F32),
            sds((2, CHIPS, fl // 2, TILE), BF),
            sds((NZL, fl, quarter), BF),
        ),
        in_specs=[ANY, ANY, VMEM, ANY],
        out_specs=(VMEM, VMEM, ANY),
        scratch_shapes=[
            pltpu.VMEM((fl, rows + 2 * TILE), BF),
            pltpu.VMEM((wchunks, rows // wchunks, 3 * TILE), BF),
            DMA, DMA((wchunks,)), DMA((CHIPS,)), DMA((CHIPS,)), DMA((2,)),
            DMA((2,)), DMA((2,)), DMA((3,)), DMA((3,)), DMA,
        ],
        compiler_params=pltpu.CompilerParams(
            collective_id=0, has_side_effects=True, vmem_limit_bytes=24 << 20
        ),
    )(features, band_weights, hub_ids.reshape(1, -1), cotangent)

    agg = pl.pallas_call(
        hub_kernel,
        name="hub",
        out_shape=sds((fl, rows), BF),
        in_specs=[SMEM, SMEM, SMEM, VMEM, VMEM, ANY],
        out_specs=VMEM,
        scratch_shapes=[
            pltpu.VMEM(tile_vals.shape, BF),
            pltpu.VMEM((CHIPS, fl, TILE), BF),
            pltpu.VMEM((blocks, fl, TILE), F32),
            DMA((16,)),
        ],
        compiler_params=pltpu.CompilerParams(vmem_limit_bytes=24 << 20),
    )(tile_rows, tile_cols, tile_counts, band, hubs, tile_vals)

    act, wg = pl.pallas_call(
        back_kernel,
        name="back",
        out_shape=(sds((fl, rows), BF), sds((NYC, 8, TILE), F32)),
        in_specs=[ANY, ANY, VMEM],
        out_specs=(ANY, VMEM),
        scratch_shapes=[
            pltpu.VMEM((cols, fl, quarter), BF),
            pltpu.VMEM((NZL, fl, quarter), BF),
            pltpu.VMEM((NZL, fl, quarter), BF),
            pltpu.VMEM((NYC, NZL, 8, TILE), F32),
            pltpu.VMEM((NYC, NZL, 8, TILE), F32),
            pltpu.VMEM((NZL, 8, TILE), F32),
            pltpu.VMEM((NZ, 8, TILE), F32),
            DMA((3,)), DMA((3,)), DMA, DMA((2, NZL)), DMA((2, NZL)), DMA((2, 2)), DMA((2, 2)), DMA,
            DMA((3,)), DMA((3,)), DMA, DMA((NYC,)), DMA((NYC,)), DMA((NZ,)), DMA((NZ,)),
            DMA((NYC,)), DMA((NYC,)),
        ],
        compiler_params=pltpu.CompilerParams(
            collective_id=1, has_side_effects=True, vmem_limit_bytes=24 << 20
        ),
    )(agg, cotg, weight.reshape(cols, fl, weight.shape[1]))
    grad = wg.reshape(4, 4, 8, TILE).transpose(0, 2, 1, 3).reshape(fl, 4 * TILE)
    return act, grad


def solution(mesh):
    in_specs = (
        P("col", "blk"),
        P("blk", None),
        P("blk"),
        P("blk"),
        P("blk"),
        P("blk", None, None),
        P("blk"),
        P(),
        P("col", "blk"),
    )
    out_specs = (P("col", "blk"), P("col", None))
    return jax.shard_map(body, mesh=mesh, in_specs=in_specs, out_specs=out_specs, check_vma=False)
```

```python
import functools

import jax
import jax.numpy as jnp
from jax import lax
from jax.experimental import pallas as pl
from jax.experimental.pallas import tpu as pltpu
from jax.sharding import PartitionSpec as P

MESH = pl.DeviceIdType.MESH
BF = jnp.bfloat16
F32 = jnp.float32
TILE = 128
NY, NZH, NC, NZL, NX = 8, 3, 2, 4, 4
CHIPS = NY * NZH
NZ = NZH * NZL
NT = (((1,), (1,)), ((), ()))
VMEM = pl.BlockSpec(memory_space=pltpu.VMEM)
ANY = pl.BlockSpec(memory_space=pl.ANY)
HBM = pl.BlockSpec(memory_space=pltpu.HBM)
SMEM = pl.BlockSpec(memory_space=pltpu.SMEM)


def rcopy(src, dst, send, recv, blk, col):
    return pltpu.make_async_remote_copy(
        src_ref=src,
        dst_ref=dst,
        send_sem=send,
        recv_sem=recv,
        device_id={"blk": blk, "col": col},
        device_id_type=MESH,
    )


def signal(sem, blk, col):
    pl.semaphore_signal(sem, inc=1, device_id={"blk": blk, "col": col}, device_id_type=MESH)


def loop(start, stop, body):
    lax.fori_loop(start, stop, lambda i, c: (body(i), c)[1], 0)


def layer_kernel(
    count, feat, bw, ids, row_ids, col_ids, tv, cot, w3, act_out, wg_out,
    xe, wv, idv, rowv, colv, tvv, cotg, w3v, band, hubs, hub, part_s, hub_sum, aggq, g, act, pres, pt, sb, qb, yb, st, zb,
    in_sem, h_send, h_recv, s_sem, e_send, e_recv, c_send, c_recv, c_loc,
    z_send, z_recv, z_loc, x_send, x_recv, r_send, r_recv, a_send, a_recv, a_loc,
    p_sem, y_send, y_recv, q_send, q_recv, o_send, o_recv, t_sem,
):
    rows = bw.shape[0]
    fl = feat.shape[0]
    blocks = rows // TILE
    quarter = rows // NZL
    per = quarter // TILE
    slots = tv.shape[0]
    b = lax.axis_index("blk")
    c = lax.axis_index("col")
    core = lax.rem(b, NC)
    chip = lax.div(b, NC)
    y = lax.div(chip, NZH)
    zh = lax.rem(chip, NZH)
    z = lax.div(c, NX)
    x = lax.rem(c, NX)
    sib = b + 1 - 2 * core
    cross = lax.rem(b + 2 * core - 1 + CHIPS * NC, CHIPS * NC)
    right = lax.rem(x + 1, NX)
    left = lax.rem(x + NX - 1, NX)
    zz_me = zh * NZL + z

    def hub_peer(d):
        return lax.rem(chip + d, CHIPS) * NC + core

    def zl(d):
        return lax.rem(z + d, NZL)

    def y_peer(d):
        return lax.rem(y + d, NY)

    def y_blk(at):
        return (at * NZH + zh) * NC + core

    def z_peer(d):
        at = lax.rem(zz_me + d, NZ)
        return lax.div(at, NZL), lax.rem(at, NZL)

    def z_dev(h, l):
        return (y * NZH + h) * NC + core, l * NX + x

    barrier = pltpu.get_barrier_semaphore()
    loop(1, CHIPS, lambda d: signal(barrier, hub_peer(d), c))
    signal(barrier, cross, c)
    for i in range(1, NZH):
        for d in range(1, NZL):
            signal(barrier, *z_dev(lax.rem(zh + i, NZH), zl(d)))
    for d in range(1, NZL):
        signal(barrier, b, zl(d) * NX + x)
    signal(barrier, b, z * NX + left)
    signal(barrier, b, z * NX + right)
    signal(barrier, sib, c)

    loads = [
        pltpu.make_async_copy(src, dst, in_sem.at[i])
        for i, (src, dst) in enumerate(
            [
                (feat, xe.at[:, pl.ds(TILE, rows)]),
                (ids, idv),
                (bw.at[pl.ds(0, rows // 2)], wv.at[pl.ds(0, rows // 2)]),
                (bw.at[pl.ds(rows // 2, rows // 2)], wv.at[pl.ds(rows // 2, rows // 2)]),
                (row_ids, rowv),
                (col_ids, colv),
                (tv, tvv),
                (w3, w3v),
            ]
        )
    ]
    for k in loads:
        k.start()

    loads[0].wait()
    loads[1].wait()
    local_ids = idv[...] - b * rows
    lanes = jnp.concatenate([local_ids, local_ids], axis=1)
    step = 256
    picked = jnp.zeros((fl, TILE), F32)
    for i in range(rows // step):
        at = lax.broadcasted_iota(jnp.int32, (step, TILE), 0) + i * step
        hot = jnp.where(at == lanes, 1.0, 0.0).astype(BF)
        picked += jnp.dot(xe[:, TILE + i * step : TILE + (i + 1) * step], hot, preferred_element_type=F32)
    half = fl // 2
    low = lax.broadcasted_iota(jnp.int32, (half, TILE), 1) < TILE // 2
    hubs[0, chip] = jnp.where(low, picked[:half], picked[half:]).astype(BF)

    pl.semaphore_wait(barrier, CHIPS - 1 + 1 + (NZH - 1) * (NZL - 1) + NZL - 1 + 2 + 1)

    def hub_copy(d):
        return rcopy(hubs.at[0, chip], hubs.at[0, chip], h_send.at[d], h_recv.at[d], hub_peer(d), c)

    loop(1, CHIPS, lambda d: hub_copy(d).start())
    end = (blocks - 1) * TILE
    to_sib = rcopy(
        feat.at[:, pl.ds(pl.multiple_of((1 - core) * end, TILE), TILE)],
        xe.at[:, pl.ds(pl.multiple_of(core * (rows + TILE), TILE), TILE)],
        e_send.at[0], e_recv.at[0], sib, c,
    )
    to_cross = rcopy(
        feat.at[:, pl.ds(pl.multiple_of(core * end, TILE), TILE)],
        xe.at[:, pl.ds(pl.multiple_of((1 - core) * (rows + TILE), TILE), TILE)],
        e_send.at[1], e_recv.at[1], cross, c,
    )
    to_cross.start()
    to_sib.start()

    def part(ref, q):
        return ref.at[:, pl.ds(pl.multiple_of(q * quarter, TILE), quarter)]

    cots = [
        rcopy(part(cot, zl(d)), cotg.at[z], c_send.at[d - 1], c_recv.at[d - 1], b, zl(d) * NX + x)
        for d in range(1, NZL)
    ]
    for k in cots:
        k.start()
    own_cot = pltpu.make_async_copy(part(cot, z), cotg.at[z], c_loc)
    own_cot.start()

    def do_band(r):
        band[r] = lax.dot_general(
            xe[:, r * TILE : (r + 3) * TILE], wv[r * TILE : (r + 1) * TILE, :], NT, preferred_element_type=F32
        )

    loads[2].wait()
    loads[3].wait()
    for r in range(1, blocks - 1):
        do_band(r)
    for k in loads[4:]:
        k.wait()
    same = lax.broadcasted_iota(jnp.int32, (blocks, slots), 0) == rowv[...] - b * blocks
    used = lax.broadcasted_iota(jnp.int32, (blocks, slots), 1) < count[0]
    place = jnp.where(same & used, 1.0, 0.0).astype(BF)
    place = jnp.concatenate([place, place], axis=1)

    loop(1, CHIPS, lambda d: hub_copy(d).wait_recv())
    swap = rcopy(hubs.at[0], hubs.at[1], s_sem.at[0], s_sem.at[1], sib, c)
    swap.start()
    to_cross.wait_recv()
    to_sib.wait_recv()
    do_band(0)
    do_band(blocks - 1)
    swap.wait_recv()

    mine = hubs[0].astype(F32)
    other = hubs[1].astype(F32)
    first = jnp.where(core == 0, mine, other)
    second = jnp.where(core == 0, other, mine)
    low3 = lax.broadcasted_iota(jnp.int32, mine.shape, 2) < TILE // 2
    hub[:, :half, :] = jnp.where(low3, first, pltpu.roll(second, TILE // 2, 2)).astype(BF)
    hub[:, half:, :] = jnp.where(low3, pltpu.roll(first, TILE // 2, 2), second).astype(BF)

    def some_slots(i):
        for j in range(8):
            s = i * 8 + j
            part_s[pl.ds(s, fl, stride=slots), :] = lax.dot_general(
                hub[colv[s]], tvv[s], NT, preferred_element_type=F32
            )

    loop(0, slots // 8, some_slots)
    for f in range(fl):
        value = part_s[f * slots : (f + 1) * slots, :]
        high = value.astype(BF)
        rest = (value - high.astype(F32)).astype(BF)
        hub_sum[pl.ds(f, blocks, stride=fl), :] = jnp.dot(
            place, jnp.concatenate([high, rest], axis=0), preferred_element_type=F32
        )

    def round_part(q):
        for j in range(per):
            r = q * per + j
            at = pl.ds(pl.multiple_of(r * fl, fl), fl)
            aggq[q, :, j * TILE : (j + 1) * TILE] = (band[r] + hub_sum[at, :]).astype(BF)

    zc = [
        rcopy(aggq.at[zl(d)], g.at[c], z_send.at[d - 1], z_recv.at[d - 1], b, zl(d) * NX + x)
        for d in range(1, NZL)
    ]
    for d in (2, 1, 3):
        round_part(zl(d))
        zc[d - 1].start()
    round_part(z)
    own = pltpu.make_async_copy(aggq.at[z], g.at[c], z_loc)
    own.start()

    def x_copy(src_z, src_x, to, send, recv):
        slot = src_z * NX + src_x
        return rcopy(g.at[slot], g.at[slot], send, recv, b, z * NX + to)

    def push(d):
        src = lax.rem(z + NZL - d, NZL)
        x_copy(src, x, right, x_send.at[0, src], x_recv.at[0, src]).start()
        x_copy(src, x, left, x_send.at[1, src], x_recv.at[1, src]).start()

    own.wait()
    push(0)
    for d in (1, 3, 2):
        zc[d - 1].wait_recv()
        push(d)
    for s in range(NZL // 2):
        t = s + NZL // 2
        x_copy(s, left, right, x_send.at[0, s], x_recv.at[0, s]).wait_recv()
        x_copy(s, left, right, r_send.at[0, s], r_recv.at[0, s]).start()
        x_copy(t, right, left, x_send.at[1, t], x_recv.at[1, t]).wait_recv()
        x_copy(t, right, left, r_send.at[1, s], r_recv.at[1, s]).start()
    for k in cots:
        k.wait_recv()
    own_cot.wait()
    for s in range(NZL // 2):
        t = s + NZL // 2
        x_copy(t, left, right, x_send.at[0, t], x_recv.at[0, t]).wait_recv()
        x_copy(s, right, left, x_send.at[1, s], x_recv.at[1, s]).wait_recv()
    for s in range(NZL // 2):
        x_copy(s, left, right, r_send.at[0, s], r_recv.at[0, s]).wait_recv()
        x_copy(s, left, right, r_send.at[1, s], r_recv.at[1, s]).wait_recv()

    feats = NZL * NX * fl
    mix = jnp.concatenate([w3v[s * NX + x] for s in range(NZL)], axis=0)
    wide = 256
    for n in range(quarter // wide):
        cut = slice(n * wide, (n + 1) * wide)
        pre = jnp.dot(mix, g[:, :, cut].reshape(feats, wide), preferred_element_type=F32)
        sig = jax.nn.sigmoid(pre)
        act[:, :, cut] = (pre * sig).astype(BF).reshape(NZL, fl, wide)
        grad_in = cotg[:, :, cut].reshape(NZL * fl, wide).astype(F32)
        pres[:, cut] = (grad_in * sig * (1.0 + pre * (1.0 - sig))).astype(BF)

    ac = [
        rcopy(act.at[zl(d)], part(act_out, z), a_send.at[d - 1], a_recv.at[d - 1], b, zl(d) * NX + x)
        for d in range(1, NZL)
    ]
    halves = NZL * NX // NC

    def grad_half(h):
        cols = g[pl.ds(h * halves, halves)].reshape(halves * fl, quarter)
        got = lax.dot_general(pres[...], cols, NT, preferred_element_type=F32)
        for s in range(NZL):
            for j in range(NY):
                rt, lt = divmod(j, 2)
                pt[h, j, s] = got[s * fl + rt * 8 : s * fl + (rt + 1) * 8, lt * TILE : (lt + 1) * TILE]

    grad_half(1 - core)
    pair = rcopy(pt.at[1 - core], sb, p_sem.at[0], p_sem.at[1], sib, c)
    pair.start()
    for k in ac:
        k.start()
    own_act = pltpu.make_async_copy(act.at[z], part(act_out, z), a_loc)
    own_act.start()
    grad_half(core)
    pair.wait_recv()
    qb[...] = pt[core] + sb[...]

    def y_copy(d):
        return rcopy(qb.at[y_peer(d)], yb.at[d], y_send.at[d], y_recv.at[d], y_blk(y_peer(d)), c)

    loop(1, NY, lambda d: y_copy(d).start())
    loop(1, NY, lambda d: y_copy(d).wait_recv())
    total = qb[y]
    for d in range(1, NY):
        total = total + yb[d]
    st[...] = total

    def q_copy(d):
        return rcopy(st.at[z_peer(d)[1]], zb.at[d], q_send.at[d], q_recv.at[d], *z_dev(*z_peer(d)))

    loop(1, NZ, lambda d: q_copy(d).start())
    loop(1, NZ, lambda d: q_copy(d).wait_recv())
    tile = st[z]
    for d in range(1, NZ):
        tile = tile + zb[d]
    wg_out[core, y] = tile

    def o_copy(d):
        return rcopy(wg_out.at[core, y], wg_out.at[core, y], o_send.at[d], o_recv.at[d], y_blk(y_peer(d)), c)

    loop(1, NY, lambda d: o_copy(d).start())
    loop(1, NY, lambda d: o_copy(d).wait_recv())
    last = rcopy(wg_out.at[core], wg_out.at[core], t_sem.at[0], t_sem.at[1], sib, c)
    last.start()

    loop(1, CHIPS, lambda d: hub_copy(d).wait_send())
    swap.wait_send()
    to_cross.wait_send()
    to_sib.wait_send()
    for k in cots + zc:
        k.wait_send()
    for s in range(NZL):
        x_copy(s, x, right, x_send.at[0, s], x_recv.at[0, s]).wait_send()
        x_copy(s, x, left, x_send.at[1, s], x_recv.at[1, s]).wait_send()
    for s in range(NZL // 2):
        x_copy(s, left, right, r_send.at[0, s], r_recv.at[0, s]).wait_send()
        x_copy(s, left, left, r_send.at[1, s], r_recv.at[1, s]).wait_send()
    pair.wait_send()
    for k in ac:
        k.wait_send()
    loop(1, NY, lambda d: y_copy(d).wait_send())
    loop(1, NZ, lambda d: q_copy(d).wait_send())
    loop(1, NY, lambda d: o_copy(d).wait_send())
    for k in ac:
        k.wait_recv()
    own_act.wait()
    last.wait()


DMA = pltpu.SemaphoreType.DMA


def body(
    features, band_weights, hub_ids, tile_rows, tile_cols, tile_vals, tile_counts, weight, cotangent
):
    fl, rows = features.shape
    blocks = rows // TILE
    quarter = rows // NZL
    slots = tile_vals.shape[0]
    cols = NZL * NX
    sds = jax.ShapeDtypeStruct
    act, wg = pl.pallas_call(
        layer_kernel,
        name="layer",
        out_shape=(sds((fl, rows), BF), sds((NC, NY, 8, TILE), F32)),
        in_specs=[SMEM] + [HBM] * 8,
        out_specs=(ANY, VMEM),
        scratch_shapes=[
            pltpu.VMEM((fl, rows + 2 * TILE), BF),
            pltpu.VMEM((rows, 3 * TILE), BF),
            pltpu.VMEM((1, hub_ids.shape[0]), jnp.int32),
            pltpu.VMEM((1, slots), jnp.int32),
            pltpu.SMEM((slots,), jnp.int32),
            pltpu.VMEM(tile_vals.shape, BF),
            pltpu.VMEM((NZL, fl, quarter), BF),
            pltpu.VMEM((cols, fl, weight.shape[1]), BF),
            pltpu.VMEM((blocks, fl, TILE), F32),
            pltpu.VMEM((2, CHIPS, fl // 2, TILE), BF),
            pltpu.VMEM((CHIPS, fl, TILE), BF),
            pltpu.VMEM((fl * slots, TILE), F32),
            pltpu.VMEM((blocks * fl, TILE), F32),
            pltpu.VMEM((NZL, fl, quarter), BF),
            pltpu.VMEM((cols, fl, quarter), BF),
            pltpu.VMEM((NZL, fl, quarter), BF),
            pltpu.VMEM((NZL * fl, quarter), BF),
            pltpu.VMEM((NC, NY, NZL, 8, TILE), F32),
            pltpu.VMEM((NY, NZL, 8, TILE), F32),
            pltpu.VMEM((NY, NZL, 8, TILE), F32),
            pltpu.VMEM((NY, NZL, 8, TILE), F32),
            pltpu.VMEM((NZL, 8, TILE), F32),
            pltpu.VMEM((NZ, 8, TILE), F32),
            DMA((8,)), DMA((CHIPS,)), DMA((CHIPS,)), DMA((2,)), DMA((2,)), DMA((2,)), DMA((3,)), DMA((3,)), DMA,
            DMA((3,)), DMA((3,)), DMA, DMA((2, NZL)), DMA((2, NZL)), DMA((2, 2)), DMA((2, 2)), DMA((3,)), DMA((3,)), DMA,
            DMA((2,)), DMA((NY,)), DMA((NY,)), DMA((NZ,)), DMA((NZ,)), DMA((NY,)), DMA((NY,)), DMA((2,)),
        ],
        compiler_params=pltpu.CompilerParams(
            collective_id=0, has_side_effects=True, vmem_limit_bytes=60 << 20
        ),
    )(
        tile_counts, features, band_weights, hub_ids.reshape(1, -1), tile_rows.reshape(1, -1), tile_cols,
        tile_vals, cotangent, weight.reshape(cols, fl, weight.shape[1]),
    )
    grad = wg.reshape(NC, 4, 2, 8, TILE).transpose(1, 3, 0, 2, 4).reshape(fl, 4 * TILE)
    return act, grad


def solution(mesh):
    in_specs = (
        P("col", "blk"),
        P("blk", None),
        P("blk"),
        P("blk"),
        P("blk"),
        P("blk", None, None),
        P("blk"),
        P(),
        P("col", "blk"),
    )
    out_specs = (P("col", "blk"), P("col", None))
    return jax.shard_map(body, mesh=mesh, in_specs=in_specs, out_specs=out_specs, check_vma=False)
```

```python
import functools

import jax
import jax.numpy as jnp
from jax import lax
from jax.experimental import pallas as pl
from jax.experimental.pallas import tpu as pltpu
from jax.sharding import PartitionSpec as P

MESH = pl.DeviceIdType.MESH
BF = jnp.bfloat16
F32 = jnp.float32
TILE = 128
NY, NZH, NC, NZL, NX = 8, 3, 2, 4, 4
CHIPS = NY * NZH
NZ = NZH * NZL
NT = (((1,), (1,)), ((), ()))
VMEM = pl.BlockSpec(memory_space=pltpu.VMEM)
ANY = pl.BlockSpec(memory_space=pl.ANY)
HBM = pl.BlockSpec(memory_space=pltpu.HBM)
SMEM = pl.BlockSpec(memory_space=pltpu.SMEM)


def rcopy(src, dst, send, recv, blk, col):
    return pltpu.make_async_remote_copy(
        src_ref=src,
        dst_ref=dst,
        send_sem=send,
        recv_sem=recv,
        device_id={"blk": blk, "col": col},
        device_id_type=MESH,
    )


def signal(sem, blk, col):
    pl.semaphore_signal(sem, inc=1, device_id={"blk": blk, "col": col}, device_id_type=MESH)


def far_first(count):
    return sorted(range(1, count), key=lambda d: (-min(d, count - d), d))


def loop(start, stop, body):
    lax.fori_loop(start, stop, lambda i, c: (body(i), c)[1], 0)


def layer_kernel(
    count, feat, bw, ids, row_ids, col_ids, tv, cot, w3, act_out, wg_out,
    xe, wv, idv, rowv, colv, tvv, cotg, w3v, band, hubs, hub, part_s, hub_sum, aggq, g, act, pres, pt, sb, qb, yb, st, zb,
    in_sem, h_send, h_recv, s_sem, e_send, e_recv, c_send, c_recv, c_loc,
    z_send, z_recv, x_send, x_recv, r_send, r_recv, a_send, a_recv, a_loc,
    p_sem, y_send, y_recv, q_send, q_recv, o_send, o_recv, t_sem,
):
    rows = bw.shape[0]
    fl = feat.shape[0]
    blocks = rows // TILE
    quarter = rows // NZL
    per = quarter // TILE
    slots = tv.shape[0]
    b = lax.axis_index("blk")
    c = lax.axis_index("col")
    core = lax.rem(b, NC)
    chip = lax.div(b, NC)
    y = lax.div(chip, NZH)
    zh = lax.rem(chip, NZH)
    z = lax.div(c, NX)
    x = lax.rem(c, NX)
    sib = b + 1 - 2 * core
    cross = lax.rem(b + 2 * core - 1 + CHIPS * NC, CHIPS * NC)
    right = lax.rem(x + 1, NX)
    left = lax.rem(x + NX - 1, NX)
    zz_me = zh * NZL + z

    def hub_peer(d):
        return lax.rem(chip + d, CHIPS) * NC + core

    def zl(d):
        return lax.rem(z + d, NZL)

    def y_peer(d):
        return lax.rem(y + d, NY)

    def y_blk(at):
        return (at * NZH + zh) * NC + core

    def z_peer(d):
        at = lax.rem(zz_me + d, NZ)
        return lax.div(at, NZL), lax.rem(at, NZL)

    def z_dev(h, l):
        return (y * NZH + h) * NC + core, l * NX + x

    loads = [
        pltpu.make_async_copy(src, dst, in_sem.at[i])
        for i, (src, dst) in enumerate(
            [
                (feat, xe.at[:, pl.ds(TILE, rows)]),
                (ids, idv),
                (bw.at[pl.ds(0, rows // 2)], wv.at[pl.ds(0, rows // 2)]),
                (bw.at[pl.ds(rows // 2, rows // 2)], wv.at[pl.ds(rows // 2, rows // 2)]),
                (row_ids, rowv),
                (col_ids, colv),
                (tv, tvv),
                (w3, w3v),
            ]
        )
    ]
    loads[0].start()
    loads[1].start()
    barrier = pltpu.get_barrier_semaphore()
    for d in far_first(CHIPS):
        signal(barrier, hub_peer(d), c)
    signal(barrier, cross, c)
    for i in range(1, NZH):
        for d in range(1, NZL):
            signal(barrier, *z_dev(lax.rem(zh + i, NZH), zl(d)))
    for d in range(1, NZL):
        signal(barrier, b, zl(d) * NX + x)
    signal(barrier, b, z * NX + left)
    signal(barrier, b, z * NX + right)
    signal(barrier, sib, c)
    for k in loads[2:]:
        k.start()

    loads[0].wait()
    loads[1].wait()
    local_ids = idv[...] - b * rows
    lanes = jnp.concatenate([local_ids, local_ids], axis=1)
    step = 256
    picked = jnp.zeros((fl, TILE), F32)
    for i in range(rows // step):
        at = lax.broadcasted_iota(jnp.int32, (step, TILE), 0) + i * step
        hot = jnp.where(at == lanes, 1.0, 0.0).astype(BF)
        picked += jnp.dot(xe[:, TILE + i * step : TILE + (i + 1) * step], hot, preferred_element_type=F32)
    half = fl // 2
    low = lax.broadcasted_iota(jnp.int32, (half, TILE), 1) < TILE // 2
    hubs[0, chip] = jnp.where(low, picked[:half], picked[half:]).astype(BF)

    pl.semaphore_wait(barrier, CHIPS - 1 + 1 + (NZH - 1) * (NZL - 1) + NZL - 1 + 2 + 1)

    def hub_copy(d):
        return rcopy(hubs.at[0, chip], hubs.at[0, chip], h_send.at[d], h_recv.at[d], hub_peer(d), c)

    for d in far_first(CHIPS):
        hub_copy(d).start()
    end = (blocks - 1) * TILE
    to_sib = rcopy(
        feat.at[:, pl.ds(pl.multiple_of((1 - core) * end, TILE), TILE)],
        xe.at[:, pl.ds(pl.multiple_of(core * (rows + TILE), TILE), TILE)],
        e_send.at[0], e_recv.at[0], sib, c,
    )
    to_cross = rcopy(
        feat.at[:, pl.ds(pl.multiple_of(core * end, TILE), TILE)],
        xe.at[:, pl.ds(pl.multiple_of((1 - core) * (rows + TILE), TILE), TILE)],
        e_send.at[1], e_recv.at[1], cross, c,
    )
    to_cross.start()
    to_sib.start()

    def part(ref, q):
        return ref.at[:, pl.ds(pl.multiple_of(q * quarter, TILE), quarter)]

    cots = [
        rcopy(part(cot, zl(d)), cotg.at[z], c_send.at[d - 1], c_recv.at[d - 1], b, zl(d) * NX + x)
        for d in range(1, NZL)
    ]
    for k in cots:
        k.start()
    own_cot = pltpu.make_async_copy(part(cot, z), cotg.at[z], c_loc)
    own_cot.start()

    def do_band(r):
        band[r] = lax.dot_general(
            xe[:, r * TILE : (r + 3) * TILE], wv[r * TILE : (r + 1) * TILE, :], NT, preferred_element_type=F32
        )

    loads[2].wait()
    loads[3].wait()
    for r in range(1, blocks - 1):
        do_band(r)
    for k in loads[4:]:
        k.wait()
    same = lax.broadcasted_iota(jnp.int32, (blocks, slots), 0) == rowv[...] - b * blocks
    used = lax.broadcasted_iota(jnp.int32, (blocks, slots), 1) < count[0]
    place = jnp.where(same & used, 1.0, 0.0).astype(BF)
    place = jnp.concatenate([place, place], axis=1)

    loop(1, CHIPS, lambda d: hub_copy(d).wait_recv())
    swap = rcopy(hubs.at[0], hubs.at[1], s_sem.at[0], s_sem.at[1], sib, c)
    swap.start()
    to_cross.wait_recv()
    to_sib.wait_recv()
    do_band(0)
    do_band(blocks - 1)
    swap.wait_recv()

    mine = hubs[0].astype(F32)
    other = hubs[1].astype(F32)
    first = jnp.where(core == 0, mine, other)
    second = jnp.where(core == 0, other, mine)
    low3 = lax.broadcasted_iota(jnp.int32, mine.shape, 2) < TILE // 2
    hub[:, :half, :] = jnp.where(low3, first, pltpu.roll(second, TILE // 2, 2)).astype(BF)
    hub[:, half:, :] = jnp.where(low3, pltpu.roll(first, TILE // 2, 2), second).astype(BF)

    def some_pairs(i):
        for j in range(16):
            s = (i * 16 + j) * 2
            two = jnp.concatenate([hub[colv[s]], hub[colv[s + 1]]], axis=0)
            tiles = tvv[pl.ds(s, 2)].reshape(2 * TILE, TILE)
            got = lax.dot_general(two, tiles, NT, preferred_element_type=F32)
            part_s[pl.ds(s, fl, stride=slots), :] = got[:fl, :TILE]
            part_s[pl.ds(s + 1, fl, stride=slots), :] = got[fl:, TILE:]

    loop(0, slots // 32, some_pairs)
    for f in range(fl):
        value = part_s[f * slots : (f + 1) * slots, :]
        high = value.astype(BF)
        rest = (value - high.astype(F32)).astype(BF)
        hub_sum[pl.ds(f, blocks, stride=fl), :] = jnp.dot(
            place, jnp.concatenate([high, rest], axis=0), preferred_element_type=F32
        )

    wide = quarter // 2

    def side(ref, h):
        return ref.at[:, pl.ds(h * wide, wide)]

    def rounded(r):
        at = pl.ds(pl.multiple_of(r * fl, fl), fl)
        return (band[r] + hub_sum[at, :]).astype(BF)

    def z_copy(d, h):
        i = h * (NZL - 1) + d - 1
        return rcopy(side(aggq.at[zl(d)], h), side(g.at[c], h), z_send.at[i], z_recv.at[i], b, zl(d) * NX + x)

    def x_copy(src_z, src_x, h, to, way):
        slot = side(g.at[src_z * NX + src_x], h)
        return rcopy(slot, slot, x_send.at[way, h, src_z], x_recv.at[way, h, src_z], b, z * NX + to)

    def relay(src_z, h):
        origin, to = (left, right) if h == 0 else (right, left)
        slot = side(g.at[src_z * NX + origin], h)
        return rcopy(slot, slot, r_send.at[h, src_z], r_recv.at[h, src_z], b, z * NX + to)

    def source(d):
        return lax.rem(z + NZL - d, NZL)

    def push(d, h):
        x_copy(source(d), x, h, right, 0).start()
        x_copy(source(d), x, h, left, 1).start()

    def pass_on(d, h):
        x_copy(source(d), x, h, right, h).wait_recv()
        relay(source(d), h).start()

    turns = (1, 3, 2)
    for d in (2, 1, 3):
        for j in range(per):
            aggq[zl(d), :, j * TILE : (j + 1) * TILE] = rounded(zl(d) * per + j)
        z_copy(d, 0).start()
    for j in range(per):
        g[c, :, j * TILE : (j + 1) * TILE] = rounded(z * per + j)
    push(0, 0)
    for d in (2, 1, 3):
        z_copy(d, 1).start()
    push(0, 1)
    for n, d in enumerate(turns):
        z_copy(d, 0).wait_recv()
        push(d, 0)
        if n == 0:
            pass_on(0, 0)
        if n == 1:
            pass_on(0, 1)
    for d in turns:
        z_copy(d, 1).wait_recv()
        push(d, 1)
        pass_on(d, 0)
    for d in turns:
        pass_on(d, 1)
    for k in cots:
        k.wait_recv()
    own_cot.wait()

    feats = NZL * NX * fl
    mix = jnp.concatenate([w3v[s * NX + x] for s in range(NZL)], axis=0)

    def a_copy(d, h):
        i = h * (NZL - 1) + d - 1
        return rcopy(side(act.at[zl(d)], h), side(part(act_out, z), h), a_send.at[i], a_recv.at[i], b, zl(d) * NX + x)

    def own_act(h):
        return pltpu.make_async_copy(side(act.at[z], h), side(part(act_out, z), h), a_loc.at[h])

    step = 256
    for h in range(2):
        for d in range(NZL):
            x_copy(source(d), x, h, right, 1 - h).wait_recv()
            relay(source(d), h).wait_recv()
        for n in range(h * wide // step, (h + 1) * wide // step):
            cut = slice(n * step, (n + 1) * step)
            pre = jnp.dot(mix, g[:, :, cut].reshape(feats, step), preferred_element_type=F32)
            sig = jax.nn.sigmoid(pre)
            act[:, :, cut] = (pre * sig).astype(BF).reshape(NZL, fl, step)
            grad_in = cotg[:, :, cut].reshape(NZL * fl, step).astype(F32)
            pres[:, cut] = (grad_in * sig * (1.0 + pre * (1.0 - sig))).astype(BF)
        if h == 0:
            for d in range(1, NZL):
                a_copy(d, h).start()
            own_act(h).start()

    halves = NZL * NX // NC

    def grad_half(h):
        cols = g[pl.ds(h * halves, halves)].reshape(halves * fl, quarter)
        got = lax.dot_general(pres[...], cols, NT, preferred_element_type=F32)
        for s in range(NZL):
            for j in range(NY):
                rt, lt = divmod(j, 2)
                pt[h, j, s] = got[s * fl + rt * 8 : s * fl + (rt + 1) * 8, lt * TILE : (lt + 1) * TILE]

    grad_half(1 - core)
    pair = rcopy(pt.at[1 - core], sb, p_sem.at[0], p_sem.at[1], sib, c)
    pair.start()
    for d in range(1, NZL):
        a_copy(d, 1).start()
    own_act(1).start()
    grad_half(core)
    pair.wait_recv()
    qb[...] = pt[core] + sb[...]

    def y_copy(d):
        return rcopy(qb.at[y_peer(d)], yb.at[d], y_send.at[d], y_recv.at[d], y_blk(y_peer(d)), c)

    for d in far_first(NY):
        y_copy(d).start()
    loop(1, NY, lambda d: y_copy(d).wait_recv())
    total = qb[y]
    for d in range(1, NY):
        total = total + yb[d]
    st[...] = total

    def q_copy(d):
        return rcopy(st.at[z_peer(d)[1]], zb.at[d], q_send.at[d], q_recv.at[d], *z_dev(*z_peer(d)))

    for d in far_first(NZ):
        q_copy(d).start()
    loop(1, NZ, lambda d: q_copy(d).wait_recv())
    tile = st[z]
    for d in range(1, NZ):
        tile = tile + zb[d]
    wg_out[core, y] = tile

    def o_copy(d):
        return rcopy(wg_out.at[core, y], wg_out.at[core, y], o_send.at[d], o_recv.at[d], y_blk(y_peer(d)), c)

    for d in far_first(NY):
        o_copy(d).start()
    loop(1, NY, lambda d: o_copy(d).wait_recv())
    last = rcopy(wg_out.at[core], wg_out.at[core], t_sem.at[0], t_sem.at[1], sib, c)
    last.start()

    loop(1, CHIPS, lambda d: hub_copy(d).wait_send())
    swap.wait_send()
    to_cross.wait_send()
    to_sib.wait_send()
    for k in cots:
        k.wait_send()
    for h in range(2):
        for d in range(1, NZL):
            z_copy(d, h).wait_send()
        for d in range(NZL):
            x_copy(source(d), x, h, right, 0).wait_send()
            x_copy(source(d), x, h, left, 1).wait_send()
            relay(source(d), h).wait_send()
        for d in range(1, NZL):
            a_copy(d, h).wait_send()
            a_copy(d, h).wait_recv()
        own_act(h).wait()
    pair.wait_send()
    loop(1, NY, lambda d: y_copy(d).wait_send())
    loop(1, NZ, lambda d: q_copy(d).wait_send())
    loop(1, NY, lambda d: o_copy(d).wait_send())
    last.wait()


DMA = pltpu.SemaphoreType.DMA


def body(
    features, band_weights, hub_ids, tile_rows, tile_cols, tile_vals, tile_counts, weight, cotangent
):
    fl, rows = features.shape
    blocks = rows // TILE
    quarter = rows // NZL
    slots = tile_vals.shape[0]
    cols = NZL * NX
    sds = jax.ShapeDtypeStruct
    act, wg = pl.pallas_call(
        layer_kernel,
        name="layer",
        out_shape=(sds((fl, rows), BF), sds((NC, NY, 8, TILE), F32)),
        in_specs=[SMEM] + [HBM] * 8,
        out_specs=(ANY, VMEM),
        scratch_shapes=[
            pltpu.VMEM((fl, rows + 2 * TILE), BF),
            pltpu.VMEM((rows, 3 * TILE), BF),
            pltpu.VMEM((1, hub_ids.shape[0]), jnp.int32),
            pltpu.VMEM((1, slots), jnp.int32),
            pltpu.SMEM((slots,), jnp.int32),
            pltpu.VMEM(tile_vals.shape, BF),
            pltpu.VMEM((NZL, fl, quarter), BF),
            pltpu.VMEM((cols, fl, weight.shape[1]), BF),
            pltpu.VMEM((blocks, fl, TILE), F32),
            pltpu.VMEM((2, CHIPS, fl // 2, TILE), BF),
            pltpu.VMEM((CHIPS, fl, TILE), BF),
            pltpu.VMEM((fl * slots, TILE), F32),
            pltpu.VMEM((blocks * fl, TILE), F32),
            pltpu.VMEM((NZL, fl, quarter), BF),
            pltpu.VMEM((cols, fl, quarter), BF),
            pltpu.VMEM((NZL, fl, quarter), BF),
            pltpu.VMEM((NZL * fl, quarter), BF),
            pltpu.VMEM((NC, NY, NZL, 8, TILE), F32),
            pltpu.VMEM((NY, NZL, 8, TILE), F32),
            pltpu.VMEM((NY, NZL, 8, TILE), F32),
            pltpu.VMEM((NY, NZL, 8, TILE), F32),
            pltpu.VMEM((NZL, 8, TILE), F32),
            pltpu.VMEM((NZ, 8, TILE), F32),
            DMA((8,)), DMA((CHIPS,)), DMA((CHIPS,)), DMA((2,)), DMA((2,)), DMA((2,)), DMA((3,)), DMA((3,)), DMA,
            DMA((6,)), DMA((6,)), DMA((2, 2, NZL)), DMA((2, 2, NZL)), DMA((2, NZL)), DMA((2, NZL)), DMA((6,)), DMA((6,)), DMA((2,)),
            DMA((2,)), DMA((NY,)), DMA((NY,)), DMA((NZ,)), DMA((NZ,)), DMA((NY,)), DMA((NY,)), DMA((2,)),
        ],
        compiler_params=pltpu.CompilerParams(
            collective_id=0, has_side_effects=True, vmem_limit_bytes=60 << 20
        ),
    )(
        tile_counts, features, band_weights, hub_ids.reshape(1, -1), tile_rows.reshape(1, -1), tile_cols,
        tile_vals, cotangent, weight.reshape(cols, fl, weight.shape[1]),
    )
    grad = wg.reshape(NC, 4, 2, 8, TILE).transpose(1, 3, 0, 2, 4).reshape(fl, 4 * TILE)
    return act, grad


def solution(mesh):
    in_specs = (
        P("col", "blk"),
        P("blk", None),
        P("blk"),
        P("blk"),
        P("blk"),
        P("blk", None, None),
        P("blk"),
        P(),
        P("col", "blk"),
    )
    out_specs = (P("col", "blk"), P("col", None))
    return jax.shard_map(body, mesh=mesh, in_specs=in_specs, out_specs=out_specs, check_vma=False)
```

```python
import functools

import jax
import jax.numpy as jnp
from jax import lax
from jax.experimental import pallas as pl
from jax.experimental.pallas import tpu as pltpu
from jax.sharding import PartitionSpec as P

MESH = pl.DeviceIdType.MESH
BF = jnp.bfloat16
F32 = jnp.float32
TILE = 128
NY, NZH, NC, NZL, NX = 8, 3, 2, 4, 4
CHIPS = NY * NZH
NZ = NZH * NZL
NT = (((1,), (1,)), ((), ()))
VMEM = pl.BlockSpec(memory_space=pltpu.VMEM)
ANY = pl.BlockSpec(memory_space=pl.ANY)
HBM = pl.BlockSpec(memory_space=pltpu.HBM)
SMEM = pl.BlockSpec(memory_space=pltpu.SMEM)


def rcopy(src, dst, send, recv, blk, col):
    return pltpu.make_async_remote_copy(
        src_ref=src,
        dst_ref=dst,
        send_sem=send,
        recv_sem=recv,
        device_id={"blk": blk, "col": col},
        device_id_type=MESH,
    )


def signal(sem, blk, col):
    pl.semaphore_signal(sem, inc=1, device_id={"blk": blk, "col": col}, device_id_type=MESH)


def far_first(count):
    return sorted(range(1, count), key=lambda d: (-min(d, count - d), d))


def near_first(count):
    return far_first(count)[::-1]


def loop(start, stop, body):
    lax.fori_loop(start, stop, lambda i, c: (body(i), c)[1], 0)


def layer_kernel(
    count, feat, bw, ids, row_ids, col_ids, tv, cot, w3, act_out, wg_out,
    xe, wv, idv, rowv, colv, tvv, cotg, w3v, band, hubs, hub, part_s, hub_sum, aggq, g, act, pres, grads, pt, sb, qb, yb, st, zb,
    in_sem, h_send, h_recv, s_sem, e_send, e_recv, c_send, c_recv, c_loc,
    z_send, z_recv, x_send, x_recv, r_send, r_recv, a_send, a_recv, a_loc,
    p_sem, y_send, y_recv, q_send, q_recv, o_send, o_recv, t_sem,
):
    rows = bw.shape[0]
    fl = feat.shape[0]
    blocks = rows // TILE
    quarter = rows // NZL
    per = quarter // TILE
    slots = tv.shape[0]
    b = lax.axis_index("blk")
    c = lax.axis_index("col")
    core = lax.rem(b, NC)
    chip = lax.div(b, NC)
    y = lax.div(chip, NZH)
    zh = lax.rem(chip, NZH)
    z = lax.div(c, NX)
    x = lax.rem(c, NX)
    sib = b + 1 - 2 * core
    cross = lax.rem(b + 2 * core - 1 + CHIPS * NC, CHIPS * NC)
    right = lax.rem(x + 1, NX)
    left = lax.rem(x + NX - 1, NX)
    zz_me = zh * NZL + z

    def hub_peer(d):
        return lax.rem(chip + d, CHIPS) * NC + core

    def zl(d):
        return lax.rem(z + d, NZL)

    def y_peer(d):
        return lax.rem(y + d, NY)

    def y_blk(at):
        return (at * NZH + zh) * NC + core

    def z_peer(d):
        at = lax.rem(zz_me + d, NZ)
        return lax.div(at, NZL), lax.rem(at, NZL)

    def z_dev(h, l):
        return (y * NZH + h) * NC + core, l * NX + x

    loads = [
        pltpu.make_async_copy(src, dst, in_sem.at[i])
        for i, (src, dst) in enumerate(
            [
                (feat, xe.at[:, pl.ds(TILE, rows)]),
                (ids, idv),
                (bw.at[pl.ds(0, rows // 2)], wv.at[pl.ds(0, rows // 2)]),
                (bw.at[pl.ds(rows // 2, rows // 2)], wv.at[pl.ds(rows // 2, rows // 2)]),
                (row_ids, rowv),
                (col_ids, colv),
                (tv, tvv),
                (w3, w3v),
            ]
        )
    ]
    loads[0].start()
    loads[1].start()
    barrier = pltpu.get_barrier_semaphore()
    for d in far_first(CHIPS):
        signal(barrier, hub_peer(d), c)
    signal(barrier, cross, c)
    for i in range(1, NZH):
        for d in range(1, NZL):
            signal(barrier, *z_dev(lax.rem(zh + i, NZH), zl(d)))
    for d in range(1, NZL):
        signal(barrier, b, zl(d) * NX + x)
    signal(barrier, b, z * NX + left)
    signal(barrier, b, z * NX + right)
    signal(barrier, sib, c)
    for k in loads[2:]:
        k.start()

    loads[0].wait()
    loads[1].wait()
    local_ids = idv[...] - b * rows
    lanes = jnp.concatenate([local_ids, local_ids], axis=1)
    step = 256
    picked = jnp.zeros((fl, TILE), F32)
    for i in range(rows // step):
        at = lax.broadcasted_iota(jnp.int32, (step, TILE), 0) + i * step
        hot = jnp.where(at == lanes, 1.0, 0.0).astype(BF)
        picked += jnp.dot(xe[:, TILE + i * step : TILE + (i + 1) * step], hot, preferred_element_type=F32)
    half = fl // 2
    low = lax.broadcasted_iota(jnp.int32, (half, TILE), 1) < TILE // 2
    hubs[0, chip] = jnp.where(low, picked[:half], picked[half:]).astype(BF)

    pl.semaphore_wait(barrier, CHIPS - 1 + 1 + (NZH - 1) * (NZL - 1) + NZL - 1 + 2 + 1)

    def hub_copy(d):
        return rcopy(hubs.at[0, chip], hubs.at[0, chip], h_send.at[d], h_recv.at[d], hub_peer(d), c)

    for d in far_first(CHIPS):
        hub_copy(d).start()
    end = (blocks - 1) * TILE
    to_sib = rcopy(
        feat.at[:, pl.ds(pl.multiple_of((1 - core) * end, TILE), TILE)],
        xe.at[:, pl.ds(pl.multiple_of(core * (rows + TILE), TILE), TILE)],
        e_send.at[0], e_recv.at[0], sib, c,
    )
    to_cross = rcopy(
        feat.at[:, pl.ds(pl.multiple_of(core * end, TILE), TILE)],
        xe.at[:, pl.ds(pl.multiple_of((1 - core) * (rows + TILE), TILE), TILE)],
        e_send.at[1], e_recv.at[1], cross, c,
    )
    to_cross.start()
    to_sib.start()

    def part(ref, q):
        return ref.at[:, pl.ds(pl.multiple_of(q * quarter, TILE), quarter)]

    cots = [
        rcopy(part(cot, zl(d)), cotg.at[z], c_send.at[d - 1], c_recv.at[d - 1], b, zl(d) * NX + x)
        for d in range(1, NZL)
    ]
    for k in cots:
        k.start()
    own_cot = pltpu.make_async_copy(part(cot, z), cotg.at[z], c_loc)
    own_cot.start()

    def do_band(r):
        band[r] = lax.dot_general(
            xe[:, r * TILE : (r + 3) * TILE], wv[r * TILE : (r + 1) * TILE, :], NT, preferred_element_type=F32
        )

    loads[2].wait()
    loads[3].wait()
    for r in range(1, blocks - 1):
        do_band(r)
    for k in loads[4:]:
        k.wait()
    same = lax.broadcasted_iota(jnp.int32, (blocks, slots), 0) == rowv[...] - b * blocks
    used = lax.broadcasted_iota(jnp.int32, (blocks, slots), 1) < count[0]
    place = jnp.where(same & used, 1.0, 0.0).astype(BF)
    place = jnp.concatenate([place, place], axis=1)

    for d in near_first(CHIPS):
        hub_copy(d).wait_recv()
    swap = rcopy(hubs.at[0], hubs.at[1], s_sem.at[0], s_sem.at[1], sib, c)
    swap.start()
    to_cross.wait_recv()
    to_sib.wait_recv()
    do_band(0)
    do_band(blocks - 1)
    swap.wait_recv()

    mine = hubs[0].astype(F32)
    other = hubs[1].astype(F32)
    first = jnp.where(core == 0, mine, other)
    second = jnp.where(core == 0, other, mine)
    low3 = lax.broadcasted_iota(jnp.int32, mine.shape, 2) < TILE // 2
    hub[:, :half, :] = jnp.where(low3, first, pltpu.roll(second, TILE // 2, 2)).astype(BF)
    hub[:, half:, :] = jnp.where(low3, pltpu.roll(first, TILE // 2, 2), second).astype(BF)

    def some_pairs(i):
        for j in range(32):
            s = (i * 32 + j) * 2
            two = jnp.concatenate([hub[colv[s]], hub[colv[s + 1]]], axis=0)
            tiles = tvv[pl.ds(s, 2)].reshape(2 * TILE, TILE)
            got = lax.dot_general(two, tiles, NT, preferred_element_type=F32)
            part_s[pl.ds(s, fl, stride=slots), :] = got[:fl, :TILE]
            part_s[pl.ds(s + 1, fl, stride=slots), :] = got[fl:, TILE:]

    loop(0, slots // 64, some_pairs)
    for f in range(fl):
        value = part_s[f * slots : (f + 1) * slots, :]
        high = value.astype(BF)
        rest = (value - high.astype(F32)).astype(BF)
        hub_sum[pl.ds(f, blocks, stride=fl), :] = jnp.dot(
            place, jnp.concatenate([high, rest], axis=0), preferred_element_type=F32
        )

    wide = quarter // 2

    def side(ref, h):
        return ref.at[:, pl.ds(h * wide, wide)]

    def rounded(r):
        at = pl.ds(pl.multiple_of(r * fl, fl), fl)
        return (band[r] + hub_sum[at, :]).astype(BF)

    def z_copy(d, h):
        i = h * (NZL - 1) + d - 1
        return rcopy(side(aggq.at[zl(d)], h), side(g.at[c], h), z_send.at[i], z_recv.at[i], b, zl(d) * NX + x)

    def x_copy(src_z, src_x, h, to, way):
        slot = side(g.at[src_z * NX + src_x], h)
        return rcopy(slot, slot, x_send.at[way, h, src_z], x_recv.at[way, h, src_z], b, z * NX + to)

    def relay(src_z, h):
        origin, to = (left, right) if h == 0 else (right, left)
        slot = side(g.at[src_z * NX + origin], h)
        return rcopy(slot, slot, r_send.at[h, src_z], r_recv.at[h, src_z], b, z * NX + to)

    def source(d):
        return lax.rem(z + NZL - d, NZL)

    def push(d, h):
        x_copy(source(d), x, h, right, 0).start()
        x_copy(source(d), x, h, left, 1).start()

    def pass_on(d, h):
        x_copy(source(d), x, h, right, h).wait_recv()
        relay(source(d), h).start()

    turns = (1, 3, 2)
    for d in (2, 1, 3):
        for j in range(per):
            aggq[zl(d), :, j * TILE : (j + 1) * TILE] = rounded(zl(d) * per + j)
        z_copy(d, 0).start()
    for j in range(per):
        g[c, :, j * TILE : (j + 1) * TILE] = rounded(z * per + j)
    push(0, 0)
    for d in (2, 1, 3):
        z_copy(d, 1).start()
    push(0, 1)
    for n, d in enumerate(turns):
        z_copy(d, 0).wait_recv()
        push(d, 0)
        if n == 0:
            pass_on(0, 0)
        if n == 1:
            pass_on(0, 1)
    for d in turns:
        z_copy(d, 1).wait_recv()
        push(d, 1)
        pass_on(d, 0)
    for d in turns:
        pass_on(d, 1)
    for k in cots:
        k.wait_recv()
    own_cot.wait()

    feats = NZL * NX * fl
    mix = jnp.concatenate([w3v[s * NX + x] for s in range(NZL)], axis=0)

    def a_copy(d, h):
        i = h * (NZL - 1) + d - 1
        return rcopy(side(act.at[zl(d)], h), side(part(act_out, z), h), a_send.at[i], a_recv.at[i], b, zl(d) * NX + x)

    def own_act(h):
        return pltpu.make_async_copy(side(act.at[z], h), side(part(act_out, z), h), a_loc.at[h])

    halves = NZL * NX // NC

    def grad_part(k, h):
        cut = slice(h * wide, (h + 1) * wide)
        cols = g[pl.ds(k * halves, halves), :, cut].reshape(halves * fl, wide)
        return lax.dot_general(pres[:, cut], cols, NT, preferred_element_type=F32)

    step = 256
    for h in range(2):
        for d in range(NZL):
            x_copy(source(d), x, h, right, 1 - h).wait_recv()
            relay(source(d), h).wait_recv()
        for n in range(h * wide // step, (h + 1) * wide // step):
            cut = slice(n * step, (n + 1) * step)
            pre = jnp.dot(mix, g[:, :, cut].reshape(feats, step), preferred_element_type=F32)
            sig = jax.nn.sigmoid(pre)
            act[:, :, cut] = (pre * sig).astype(BF).reshape(NZL, fl, step)
            grad_in = cotg[:, :, cut].reshape(NZL * fl, step).astype(F32)
            pres[:, cut] = (grad_in * sig * (1.0 + pre * (1.0 - sig))).astype(BF)
        if h == 0:
            for d in range(1, NZL):
                a_copy(d, h).start()
            own_act(h).start()
            for k in range(NC):
                grads[k] = grad_part(k, h)


    def grad_half(k):
        got = grads[k] + grad_part(k, 1)
        for s in range(NZL):
            for j in range(NY):
                rt, lt = divmod(j, 2)
                pt[k, j, s] = got[s * fl + rt * 8 : s * fl + (rt + 1) * 8, lt * TILE : (lt + 1) * TILE]

    grad_half(1 - core)
    pair = rcopy(pt.at[1 - core], sb, p_sem.at[0], p_sem.at[1], sib, c)
    pair.start()
    for d in range(1, NZL):
        a_copy(d, 1).start()
    own_act(1).start()
    grad_half(core)
    pair.wait_recv()
    qb[...] = pt[core] + sb[...]

    def y_copy(d):
        return rcopy(qb.at[y_peer(d)], yb.at[d], y_send.at[d], y_recv.at[d], y_blk(y_peer(d)), c)

    for d in far_first(NY):
        y_copy(d).start()
    total = qb[y]
    for d in near_first(NY):
        y_copy(d).wait_recv()
        total = total + yb[d]
    st[...] = total

    def q_copy(d):
        return rcopy(st.at[z_peer(d)[1]], zb.at[d], q_send.at[d], q_recv.at[d], *z_dev(*z_peer(d)))

    for d in far_first(NZ):
        q_copy(d).start()
    tile = st[z]
    for d in near_first(NZ):
        q_copy(d).wait_recv()
        tile = tile + zb[d]
    wg_out[core, y] = tile

    def o_copy(d):
        return rcopy(wg_out.at[core, y], wg_out.at[core, y], o_send.at[d], o_recv.at[d], y_blk(y_peer(d)), c)

    for d in far_first(NY):
        o_copy(d).start()
    for d in near_first(NY):
        o_copy(d).wait_recv()
    last = rcopy(wg_out.at[core], wg_out.at[core], t_sem.at[0], t_sem.at[1], sib, c)
    last.start()

    loop(1, CHIPS, lambda d: hub_copy(d).wait_send())
    swap.wait_send()
    to_cross.wait_send()
    to_sib.wait_send()
    for k in cots:
        k.wait_send()
    for h in range(2):
        for d in range(1, NZL):
            z_copy(d, h).wait_send()
        for d in range(NZL):
            x_copy(source(d), x, h, right, 0).wait_send()
            x_copy(source(d), x, h, left, 1).wait_send()
            relay(source(d), h).wait_send()
        for d in range(1, NZL):
            a_copy(d, h).wait_send()
            a_copy(d, h).wait_recv()
        own_act(h).wait()
    pair.wait_send()
    loop(1, NY, lambda d: y_copy(d).wait_send())
    loop(1, NZ, lambda d: q_copy(d).wait_send())
    loop(1, NY, lambda d: o_copy(d).wait_send())
    last.wait()


def write_kernel(act, tiles, act_out, grad_out, sem):
    copies = [pltpu.make_async_copy(act, act_out, sem.at[NC * NY])]
    for k in range(NC):
        for j in range(NY):
            rt, lt = divmod(j, 2)
            to = grad_out.at[pl.ds(rt * 8, 8), pl.ds((k * 2 + lt) * TILE, TILE)]
            copies.append(pltpu.make_async_copy(tiles.at[k, j], to, sem.at[k * NY + j]))
    for k in copies:
        k.start()
    for k in copies:
        k.wait()


DMA = pltpu.SemaphoreType.DMA


def body(
    features, band_weights, hub_ids, tile_rows, tile_cols, tile_vals, tile_counts, weight, cotangent
):
    fl, rows = features.shape
    blocks = rows // TILE
    quarter = rows // NZL
    slots = tile_vals.shape[0]
    cols = NZL * NX
    sds = jax.ShapeDtypeStruct
    act, wg = pl.pallas_call(
        layer_kernel,
        name="layer",
        out_shape=(sds((fl, rows), BF), sds((NC, NY, 8, TILE), F32)),
        in_specs=[SMEM] + [HBM] * 8,
        out_specs=(ANY, VMEM),
        scratch_shapes=[
            pltpu.VMEM((fl, rows + 2 * TILE), BF),
            pltpu.VMEM((rows, 3 * TILE), BF),
            pltpu.VMEM((1, hub_ids.shape[0]), jnp.int32),
            pltpu.VMEM((1, slots), jnp.int32),
            pltpu.SMEM((slots,), jnp.int32),
            pltpu.VMEM(tile_vals.shape, BF),
            pltpu.VMEM((NZL, fl, quarter), BF),
            pltpu.VMEM((cols, fl, weight.shape[1]), BF),
            pltpu.VMEM((blocks, fl, TILE), F32),
            pltpu.VMEM((2, CHIPS, fl // 2, TILE), BF),
            pltpu.VMEM((CHIPS, fl, TILE), BF),
            pltpu.VMEM((fl * slots, TILE), F32),
            pltpu.VMEM((blocks * fl, TILE), F32),
            pltpu.VMEM((NZL, fl, quarter), BF),
            pltpu.VMEM((cols, fl, quarter), BF),
            pltpu.VMEM((NZL, fl, quarter), BF),
            pltpu.VMEM((NZL * fl, quarter), BF),
            pltpu.VMEM((NC, NZL * fl, cols * fl // NC), F32),
            pltpu.VMEM((NC, NY, NZL, 8, TILE), F32),
            pltpu.VMEM((NY, NZL, 8, TILE), F32),
            pltpu.VMEM((NY, NZL, 8, TILE), F32),
            pltpu.VMEM((NY, NZL, 8, TILE), F32),
            pltpu.VMEM((NZL, 8, TILE), F32),
            pltpu.VMEM((NZ, 8, TILE), F32),
            DMA((8,)), DMA((CHIPS,)), DMA((CHIPS,)), DMA((2,)), DMA((2,)), DMA((2,)), DMA((3,)), DMA((3,)), DMA,
            DMA((6,)), DMA((6,)), DMA((2, 2, NZL)), DMA((2, 2, NZL)), DMA((2, NZL)), DMA((2, NZL)), DMA((6,)), DMA((6,)), DMA((2,)),
            DMA((2,)), DMA((NY,)), DMA((NY,)), DMA((NZ,)), DMA((NZ,)), DMA((NY,)), DMA((NY,)), DMA((2,)),
        ],
        compiler_params=pltpu.CompilerParams(
            collective_id=0, has_side_effects=True, vmem_limit_bytes=40 << 20
        ),
    )(
        tile_counts,
        *(
            pltpu.with_memory_space_constraint(k, pltpu.HBM)
            for k in (
                features, band_weights, hub_ids.reshape(1, -1), tile_rows.reshape(1, -1), tile_cols,
                tile_vals, cotangent, weight.reshape(cols, fl, weight.shape[1]),
            )
        ),
    )
    return pl.pallas_call(
        write_kernel,
        name="write",
        out_shape=(sds((fl, rows), BF), sds((fl, NC * NY * 8 * TILE // fl), F32)),
        in_specs=[VMEM, VMEM],
        out_specs=(HBM, HBM),
        scratch_shapes=[DMA((1 + NC * NY,))],
    )(pltpu.with_memory_space_constraint(act, pltpu.VMEM), pltpu.with_memory_space_constraint(wg, pltpu.VMEM))


def solution(mesh):
    in_specs = (
        P("col", "blk"),
        P("blk", None),
        P("blk"),
        P("blk"),
        P("blk"),
        P("blk", None, None),
        P("blk"),
        P(),
        P("col", "blk"),
    )
    out_specs = (P("col", "blk"), P("col", None))
    return jax.shard_map(body, mesh=mesh, in_specs=in_specs, out_specs=out_specs, check_vma=False)
```

```python
import functools

import jax
import jax.numpy as jnp
from jax import lax
from jax.experimental import pallas as pl
from jax.experimental.pallas import tpu as pltpu
from jax.sharding import PartitionSpec as P

MESH = pl.DeviceIdType.MESH
BF = jnp.bfloat16
F32 = jnp.float32
TILE = 128
NY, NZH, NC, NZL, NX = 8, 3, 2, 4, 4
CHIPS = NY * NZH
NZ = NZH * NZL
NT = (((1,), (1,)), ((), ()))
VMEM = pl.BlockSpec(memory_space=pltpu.VMEM)
ANY = pl.BlockSpec(memory_space=pl.ANY)
HBM = pl.BlockSpec(memory_space=pltpu.HBM)
SMEM = pl.BlockSpec(memory_space=pltpu.SMEM)


GRAD_STEPS = sorted(
    [(d, k) for d in range(NY) for k in range(NC) if (d, k) != (0, 0)], key=lambda at: -min(at[0], NY - at[0])
)


def rcopy(src, dst, send, recv, blk, col):
    return pltpu.make_async_remote_copy(
        src_ref=src,
        dst_ref=dst,
        send_sem=send,
        recv_sem=recv,
        device_id={"blk": blk, "col": col},
        device_id_type=MESH,
    )


def signal(sem, blk, col):
    pl.semaphore_signal(sem, inc=1, device_id={"blk": blk, "col": col}, device_id_type=MESH)


def far_first(count):
    return sorted(range(1, count), key=lambda d: (-min(d, count - d), d))


def near_first(count):
    return far_first(count)[::-1]


def loop(start, stop, body):
    lax.fori_loop(start, stop, lambda i, c: (body(i), c)[1], 0)


def layer_kernel(
    count, feat, bw, ids, row_ids, col_ids, tv, cot, w3, act_out, wg_out,
    xe, wv, idv, rowv, colv, tvv, cotg, w3v, band, hubs, hub, part_s, hub_sum, aggq, g, act, pres, grads, pt, sb, qb, yb, st, zb,
    in_sem, h_send, h_recv, s_sem, e_send, e_recv, c_send, c_recv, c_loc,
    z_send, z_recv, x_send, x_recv, r_send, r_recv, a_send, a_recv, a_loc,
    p_sem, y_send, y_recv, q_send, q_recv, o_send, o_recv,
):
    rows = bw.shape[0]
    fl = feat.shape[0]
    blocks = rows // TILE
    quarter = rows // NZL
    per = quarter // TILE
    slots = tv.shape[0]
    b = lax.axis_index("blk")
    c = lax.axis_index("col")
    core = lax.rem(b, NC)
    chip = lax.div(b, NC)
    y = lax.div(chip, NZH)
    zh = lax.rem(chip, NZH)
    z = lax.div(c, NX)
    x = lax.rem(c, NX)
    sib = b + 1 - 2 * core
    cross = lax.rem(b + 2 * core - 1 + CHIPS * NC, CHIPS * NC)
    right = lax.rem(x + 1, NX)
    left = lax.rem(x + NX - 1, NX)
    zz_me = zh * NZL + z

    def hub_peer(d):
        return lax.rem(chip + d, CHIPS) * NC + core

    def y_dev(d, k):
        return (lax.rem(y + d, NY) * NZH + zh) * NC + (core if k == 0 else 1 - core)

    def zl(d):
        return lax.rem(z + d, NZL)

    def y_peer(d):
        return lax.rem(y + d, NY)

    def y_blk(at):
        return (at * NZH + zh) * NC + core

    def z_peer(d):
        at = lax.rem(zz_me + d, NZ)
        return lax.div(at, NZL), lax.rem(at, NZL)

    def z_dev(h, l):
        return (y * NZH + h) * NC + core, l * NX + x

    loads = [
        pltpu.make_async_copy(src, dst, in_sem.at[i])
        for i, (src, dst) in enumerate(
            [
                (feat, xe.at[:, pl.ds(TILE, rows)]),
                (ids, idv),
                (bw.at[pl.ds(0, rows // 2)], wv.at[pl.ds(0, rows // 2)]),
                (bw.at[pl.ds(rows // 2, rows // 2)], wv.at[pl.ds(rows // 2, rows // 2)]),
                (row_ids, rowv),
                (col_ids, colv),
                (tv, tvv),
                (w3, w3v),
            ]
        )
    ]
    loads[0].start()
    loads[1].start()
    barrier = pltpu.get_barrier_semaphore()
    for d in far_first(CHIPS):
        signal(barrier, hub_peer(d), c)
    for d in range(1, NY):
        signal(barrier, y_dev(d, 1), c)
    signal(barrier, cross, c)
    for i in range(1, NZH):
        for d in range(1, NZL):
            signal(barrier, *z_dev(lax.rem(zh + i, NZH), zl(d)))
    for d in range(1, NZL):
        signal(barrier, b, zl(d) * NX + x)
    signal(barrier, b, z * NX + left)
    signal(barrier, b, z * NX + right)
    signal(barrier, sib, c)
    for k in loads[2:]:
        k.start()

    loads[0].wait()
    loads[1].wait()
    local_ids = idv[...] - b * rows
    lanes = jnp.concatenate([local_ids, local_ids], axis=1)
    step = 256
    picked = jnp.zeros((fl, TILE), F32)
    for i in range(rows // step):
        at = lax.broadcasted_iota(jnp.int32, (step, TILE), 0) + i * step
        hot = jnp.where(at == lanes, 1.0, 0.0).astype(BF)
        picked += jnp.dot(xe[:, TILE + i * step : TILE + (i + 1) * step], hot, preferred_element_type=F32)
    half = fl // 2
    low = lax.broadcasted_iota(jnp.int32, (half, TILE), 1) < TILE // 2
    hubs[0, chip] = jnp.where(low, picked[:half], picked[half:]).astype(BF)

    pl.semaphore_wait(barrier, CHIPS - 1 + NY - 1 + 1 + (NZH - 1) * (NZL - 1) + NZL - 1 + 2 + 1)

    def hub_copy(d):
        return rcopy(hubs.at[0, chip], hubs.at[0, chip], h_send.at[d], h_recv.at[d], hub_peer(d), c)

    for d in far_first(CHIPS):
        hub_copy(d).start()
    end = (blocks - 1) * TILE
    to_sib = rcopy(
        feat.at[:, pl.ds(pl.multiple_of((1 - core) * end, TILE), TILE)],
        xe.at[:, pl.ds(pl.multiple_of(core * (rows + TILE), TILE), TILE)],
        e_send.at[0], e_recv.at[0], sib, c,
    )
    to_cross = rcopy(
        feat.at[:, pl.ds(pl.multiple_of(core * end, TILE), TILE)],
        xe.at[:, pl.ds(pl.multiple_of((1 - core) * (rows + TILE), TILE), TILE)],
        e_send.at[1], e_recv.at[1], cross, c,
    )
    to_cross.start()
    to_sib.start()

    def part(ref, q):
        return ref.at[:, pl.ds(pl.multiple_of(q * quarter, TILE), quarter)]

    cots = [
        rcopy(part(cot, zl(d)), cotg.at[z], c_send.at[d - 1], c_recv.at[d - 1], b, zl(d) * NX + x)
        for d in range(1, NZL)
    ]
    for k in cots:
        k.start()
    own_cot = pltpu.make_async_copy(part(cot, z), cotg.at[z], c_loc)
    own_cot.start()

    def do_band(r):
        band[r] = lax.dot_general(
            xe[:, r * TILE : (r + 3) * TILE], wv[r * TILE : (r + 1) * TILE, :], NT, preferred_element_type=F32
        )

    loads[2].wait()
    loads[3].wait()
    for r in range(1, blocks - 1):
        do_band(r)
    for k in loads[4:]:
        k.wait()
    same = lax.broadcasted_iota(jnp.int32, (blocks, slots), 0) == rowv[...] - b * blocks
    used = lax.broadcasted_iota(jnp.int32, (blocks, slots), 1) < count[0]
    place = jnp.where(same & used, 1.0, 0.0).astype(BF)
    place = jnp.concatenate([place, place], axis=1)

    for d in near_first(CHIPS):
        hub_copy(d).wait_recv()
    swap = rcopy(hubs.at[0], hubs.at[1], s_sem.at[0], s_sem.at[1], sib, c)
    swap.start()
    to_cross.wait_recv()
    to_sib.wait_recv()
    do_band(0)
    do_band(blocks - 1)
    swap.wait_recv()

    mine = hubs[0].astype(F32)
    other = hubs[1].astype(F32)
    first = jnp.where(core == 0, mine, other)
    second = jnp.where(core == 0, other, mine)
    low3 = lax.broadcasted_iota(jnp.int32, mine.shape, 2) < TILE // 2
    hub[:, :half, :] = jnp.where(low3, first, pltpu.roll(second, TILE // 2, 2)).astype(BF)
    hub[:, half:, :] = jnp.where(low3, pltpu.roll(first, TILE // 2, 2), second).astype(BF)

    def some_pairs(i):
        for j in range(32):
            s = (i * 32 + j) * 2
            two = jnp.concatenate([hub[colv[s]], hub[colv[s + 1]]], axis=0)
            tiles = tvv[pl.ds(s, 2)].reshape(2 * TILE, TILE)
            got = lax.dot_general(two, tiles, NT, preferred_element_type=F32)
            part_s[pl.ds(s, fl, stride=slots), :] = got[:fl, :TILE]
            part_s[pl.ds(s + 1, fl, stride=slots), :] = got[fl:, TILE:]

    loop(0, slots // 64, some_pairs)
    for f in range(fl):
        value = part_s[f * slots : (f + 1) * slots, :]
        high = value.astype(BF)
        rest = (value - high.astype(F32)).astype(BF)
        hub_sum[pl.ds(f, blocks, stride=fl), :] = jnp.dot(
            place, jnp.concatenate([high, rest], axis=0), preferred_element_type=F32
        )

    wide = quarter // 2

    def side(ref, h):
        return ref.at[:, pl.ds(h * wide, wide)]

    def rounded(r):
        at = pl.ds(pl.multiple_of(r * fl, fl), fl)
        return (band[r] + hub_sum[at, :]).astype(BF)

    def z_copy(d, h):
        i = h * (NZL - 1) + d - 1
        return rcopy(side(aggq.at[zl(d)], h), side(g.at[c], h), z_send.at[i], z_recv.at[i], b, zl(d) * NX + x)

    def x_copy(src_z, src_x, h, to, way):
        slot = side(g.at[src_z * NX + src_x], h)
        return rcopy(slot, slot, x_send.at[way, h, src_z], x_recv.at[way, h, src_z], b, z * NX + to)

    def relay(src_z, h):
        origin, to = (left, right) if h == 0 else (right, left)
        slot = side(g.at[src_z * NX + origin], h)
        return rcopy(slot, slot, r_send.at[h, src_z], r_recv.at[h, src_z], b, z * NX + to)

    def source(d):
        return lax.rem(z + NZL - d, NZL)

    def push(d, h):
        x_copy(source(d), x, h, right, 0).start()
        x_copy(source(d), x, h, left, 1).start()

    def pass_on(d, h):
        x_copy(source(d), x, h, right, h).wait_recv()
        relay(source(d), h).start()

    turns = (1, 3, 2)
    for d in (2, 1, 3):
        for j in range(per):
            aggq[zl(d), :, j * TILE : (j + 1) * TILE] = rounded(zl(d) * per + j)
        z_copy(d, 0).start()
    for j in range(per):
        g[c, :, j * TILE : (j + 1) * TILE] = rounded(z * per + j)
    push(0, 0)
    for d in (2, 1, 3):
        z_copy(d, 1).start()
    push(0, 1)
    for n, d in enumerate(turns):
        z_copy(d, 0).wait_recv()
        push(d, 0)
        if n == 0:
            pass_on(0, 0)
        if n == 1:
            pass_on(0, 1)
    for d in turns:
        z_copy(d, 1).wait_recv()
        push(d, 1)
        pass_on(d, 0)
    for d in turns:
        pass_on(d, 1)
    for k in cots:
        k.wait_recv()
    own_cot.wait()

    feats = NZL * NX * fl
    mix = jnp.concatenate([w3v[s * NX + x] for s in range(NZL)], axis=0)

    def a_copy(d, h):
        i = h * (NZL - 1) + d - 1
        return rcopy(side(act.at[zl(d)], h), side(part(act_out, z), h), a_send.at[i], a_recv.at[i], b, zl(d) * NX + x)

    def own_act(h):
        return pltpu.make_async_copy(side(act.at[z], h), side(part(act_out, z), h), a_loc.at[h])

    halves = NZL * NX // NC

    def grad_part(k, h):
        cut = slice(h * wide, (h + 1) * wide)
        cols = g[pl.ds(k * halves, halves), :, cut].reshape(halves * fl, wide)
        return lax.dot_general(pres[:, cut], cols, NT, preferred_element_type=F32)

    step = 256
    for h in range(2):
        for d in range(NZL):
            x_copy(source(d), x, h, right, 1 - h).wait_recv()
            relay(source(d), h).wait_recv()
        for n in range(h * wide // step, (h + 1) * wide // step):
            cut = slice(n * step, (n + 1) * step)
            pre = jnp.dot(mix, g[:, :, cut].reshape(feats, step), preferred_element_type=F32)
            sig = jax.nn.sigmoid(pre)
            act[:, :, cut] = (pre * sig).astype(BF).reshape(NZL, fl, step)
            grad_in = cotg[:, :, cut].reshape(NZL * fl, step).astype(F32)
            pres[:, cut] = (grad_in * sig * (1.0 + pre * (1.0 - sig))).astype(BF)
        if h == 0:
            for d in range(1, NZL):
                a_copy(d, h).start()
            own_act(h).start()
            for k in range(NC):
                grads[k] = grad_part(k, h)


    def grad_half(k):
        got = grads[k] + grad_part(k, 1)
        for s in range(NZL):
            for j in range(NY):
                rt, lt = divmod(j, 2)
                pt[k, j, s] = got[s * fl + rt * 8 : s * fl + (rt + 1) * 8, lt * TILE : (lt + 1) * TILE]

    grad_half(1 - core)
    pair = rcopy(pt.at[1 - core], sb, p_sem.at[0], p_sem.at[1], sib, c)
    pair.start()
    for d in range(1, NZL):
        a_copy(d, 1).start()
    own_act(1).start()
    grad_half(core)
    pair.wait_recv()
    qb[...] = pt[core] + sb[...]

    def y_copy(d):
        return rcopy(qb.at[y_peer(d)], yb.at[d], y_send.at[d], y_recv.at[d], y_blk(y_peer(d)), c)

    for d in far_first(NY):
        y_copy(d).start()
    total = qb[y]
    for d in near_first(NY):
        y_copy(d).wait_recv()
        total = total + yb[d]
    st[...] = total

    def q_copy(d):
        return rcopy(st.at[z_peer(d)[1]], zb.at[d], q_send.at[d], q_recv.at[d], *z_dev(*z_peer(d)))

    for d in far_first(NZ):
        q_copy(d).start()
    tile = st[z]
    for d in near_first(NZ):
        q_copy(d).wait_recv()
        tile = tile + zb[d]
    wg_out[core, y] = tile

    def o_copy(d, k):
        spot = wg_out.at[core, y]
        return rcopy(spot, spot, o_send.at[k, d], o_recv.at[k, d], y_dev(d, k), c)

    for at in GRAD_STEPS:
        o_copy(*at).start()
    for at in GRAD_STEPS[::-1]:
        o_copy(*at).wait_recv()

    loop(1, CHIPS, lambda d: hub_copy(d).wait_send())
    swap.wait_send()
    to_cross.wait_send()
    to_sib.wait_send()
    for k in cots:
        k.wait_send()
    for h in range(2):
        for d in range(1, NZL):
            z_copy(d, h).wait_send()
        for d in range(NZL):
            x_copy(source(d), x, h, right, 0).wait_send()
            x_copy(source(d), x, h, left, 1).wait_send()
            relay(source(d), h).wait_send()
        for d in range(1, NZL):
            a_copy(d, h).wait_send()
            a_copy(d, h).wait_recv()
        own_act(h).wait()
    pair.wait_send()
    loop(1, NY, lambda d: y_copy(d).wait_send())
    loop(1, NZ, lambda d: q_copy(d).wait_send())
    for at in GRAD_STEPS:
        o_copy(*at).wait_send()


def write_kernel(act, tiles, act_out, grad_out, sem):
    copies = [pltpu.make_async_copy(act, act_out, sem.at[NC * NY])]
    for k in range(NC):
        for j in range(NY):
            rt, lt = divmod(j, 2)
            to = grad_out.at[pl.ds(rt * 8, 8), pl.ds((k * 2 + lt) * TILE, TILE)]
            copies.append(pltpu.make_async_copy(tiles.at[k, j], to, sem.at[k * NY + j]))
    for k in copies:
        k.start()
    for k in copies:
        k.wait()


DMA = pltpu.SemaphoreType.DMA


def body(
    features, band_weights, hub_ids, tile_rows, tile_cols, tile_vals, tile_counts, weight, cotangent
):
    fl, rows = features.shape
    blocks = rows // TILE
    quarter = rows // NZL
    slots = tile_vals.shape[0]
    cols = NZL * NX
    sds = jax.ShapeDtypeStruct
    act, wg = pl.pallas_call(
        layer_kernel,
        name="layer",
        out_shape=(sds((fl, rows), BF), sds((NC, NY, 8, TILE), F32)),
        in_specs=[SMEM] + [HBM] * 8,
        out_specs=(ANY, VMEM),
        scratch_shapes=[
            pltpu.VMEM((fl, rows + 2 * TILE), BF),
            pltpu.VMEM((rows, 3 * TILE), BF),
            pltpu.VMEM((1, hub_ids.shape[0]), jnp.int32),
            pltpu.VMEM((1, slots), jnp.int32),
            pltpu.SMEM((slots,), jnp.int32),
            pltpu.VMEM(tile_vals.shape, BF),
            pltpu.VMEM((NZL, fl, quarter), BF),
            pltpu.VMEM((cols, fl, weight.shape[1]), BF),
            pltpu.VMEM((blocks, fl, TILE), F32),
            pltpu.VMEM((2, CHIPS, fl // 2, TILE), BF),
            pltpu.VMEM((CHIPS, fl, TILE), BF),
            pltpu.VMEM((fl * slots, TILE), F32),
            pltpu.VMEM((blocks * fl, TILE), F32),
            pltpu.VMEM((NZL, fl, quarter), BF),
            pltpu.VMEM((cols, fl, quarter), BF),
            pltpu.VMEM((NZL, fl, quarter), BF),
            pltpu.VMEM((NZL * fl, quarter), BF),
            pltpu.VMEM((NC, NZL * fl, cols * fl // NC), F32),
            pltpu.VMEM((NC, NY, NZL, 8, TILE), F32),
            pltpu.VMEM((NY, NZL, 8, TILE), F32),
            pltpu.VMEM((NY, NZL, 8, TILE), F32),
            pltpu.VMEM((NY, NZL, 8, TILE), F32),
            pltpu.VMEM((NZL, 8, TILE), F32),
            pltpu.VMEM((NZ, 8, TILE), F32),
            DMA((8,)), DMA((CHIPS,)), DMA((CHIPS,)), DMA((2,)), DMA((2,)), DMA((2,)), DMA((3,)), DMA((3,)), DMA,
            DMA((6,)), DMA((6,)), DMA((2, 2, NZL)), DMA((2, 2, NZL)), DMA((2, NZL)), DMA((2, NZL)), DMA((6,)), DMA((6,)), DMA((2,)),
            DMA((2,)), DMA((NY,)), DMA((NY,)), DMA((NZ,)), DMA((NZ,)), DMA((NC, NY)), DMA((NC, NY)),
        ],
        compiler_params=pltpu.CompilerParams(
            collective_id=0, has_side_effects=True, vmem_limit_bytes=40 << 20
        ),
    )(
        tile_counts,
        *(
            pltpu.with_memory_space_constraint(k, pltpu.HBM)
            for k in (
                features, band_weights, hub_ids.reshape(1, -1), tile_rows.reshape(1, -1), tile_cols,
                tile_vals, cotangent, weight.reshape(cols, fl, weight.shape[1]),
            )
        ),
    )
    return pl.pallas_call(
        write_kernel,
        name="write",
        out_shape=(sds((fl, rows), BF), sds((fl, NC * NY * 8 * TILE // fl), F32)),
        in_specs=[VMEM, VMEM],
        out_specs=(HBM, HBM),
        scratch_shapes=[DMA((1 + NC * NY,))],
    )(pltpu.with_memory_space_constraint(act, pltpu.VMEM), pltpu.with_memory_space_constraint(wg, pltpu.VMEM))


def solution(mesh):
    in_specs = (
        P("col", "blk"),
        P("blk", None),
        P("blk"),
        P("blk"),
        P("blk"),
        P("blk", None, None),
        P("blk"),
        P(),
        P("col", "blk"),
    )
    out_specs = (P("col", "blk"), P("col", None))
    return jax.shard_map(body, mesh=mesh, in_specs=in_specs, out_specs=out_specs, check_vma=False)
```

```python
import functools

import jax
import jax.numpy as jnp
from jax import lax
from jax.experimental import pallas as pl
from jax.experimental.pallas import tpu as pltpu
from jax.sharding import PartitionSpec as P

MESH = pl.DeviceIdType.MESH
BF = jnp.bfloat16
F32 = jnp.float32
TILE = 128
NY, NZH, NC, NZL, NX = 8, 3, 2, 4, 4
CHIPS = NY * NZH
NZ = NZH * NZL
NT = (((1,), (1,)), ((), ()))
VMEM = pl.BlockSpec(memory_space=pltpu.VMEM)
ANY = pl.BlockSpec(memory_space=pl.ANY)
HBM = pl.BlockSpec(memory_space=pltpu.HBM)
SMEM = pl.BlockSpec(memory_space=pltpu.SMEM)


GRAD_STEPS = sorted(
    [(d, k) for d in range(NY) for k in range(NC) if (d, k) != (0, 0)], key=lambda at: -min(at[0], NY - at[0])
)


def rcopy(src, dst, send, recv, blk, col):
    return pltpu.make_async_remote_copy(
        src_ref=src,
        dst_ref=dst,
        send_sem=send,
        recv_sem=recv,
        device_id={"blk": blk, "col": col},
        device_id_type=MESH,
    )


def signal(sem, blk, col):
    pl.semaphore_signal(sem, inc=1, device_id={"blk": blk, "col": col}, device_id_type=MESH)


def far_first(count):
    return sorted(range(1, count), key=lambda d: (-min(d, count - d), d))


def near_first(count):
    return far_first(count)[::-1]


def loop(start, stop, body):
    lax.fori_loop(start, stop, lambda i, c: (body(i), c)[1], 0)


def layer_kernel(
    count, feat, bw, ids, row_ids, col_ids, tv, cot, w3, act_out, wg_out,
    xe, wv, idv, rowv, colv, tvv, cotg, w3v, band, hubs, hub, part_s, hub_sum, aggq, g, act, pres, grads, pt, sb, qb, yb, st, zb,
    in_sem, h_send, h_recv, s_sem, e_send, e_recv, c_send, c_recv, c_loc,
    z_send, z_recv, x_send, x_recv, r_send, r_recv, a_send, a_recv, a_loc,
    p_sem, y_send, y_recv, q_send, q_recv, o_send, o_recv,
):
    rows = bw.shape[0]
    fl = feat.shape[0]
    blocks = rows // TILE
    quarter = rows // NZL
    per = quarter // TILE
    slots = tv.shape[0]
    b = lax.axis_index("blk")
    c = lax.axis_index("col")
    core = lax.rem(b, NC)
    chip = lax.div(b, NC)
    y = lax.div(chip, NZH)
    zh = lax.rem(chip, NZH)
    z = lax.div(c, NX)
    x = lax.rem(c, NX)
    sib = b + 1 - 2 * core
    cross = lax.rem(b + 2 * core - 1 + CHIPS * NC, CHIPS * NC)
    right = lax.rem(x + 1, NX)
    left = lax.rem(x + NX - 1, NX)
    zz_me = zh * NZL + z

    def hub_peer(d):
        return lax.rem(chip + d, CHIPS) * NC + core

    def y_dev(d, k):
        return (lax.rem(y + d, NY) * NZH + zh) * NC + (core if k == 0 else 1 - core)

    def zl(d):
        return lax.rem(z + d, NZL)

    def y_peer(d):
        return lax.rem(y + d, NY)

    def y_blk(at):
        return (at * NZH + zh) * NC + core

    def z_peer(d):
        at = lax.rem(zz_me + d, NZ)
        return lax.div(at, NZL), lax.rem(at, NZL)

    def z_dev(h, l):
        return (y * NZH + h) * NC + core, l * NX + x

    loads = [
        pltpu.make_async_copy(src, dst, in_sem.at[i])
        for i, (src, dst) in enumerate(
            [
                (feat, xe.at[:, pl.ds(TILE, rows)]),
                (ids, idv),
                (bw.at[pl.ds(0, rows // 2)], wv.at[pl.ds(0, rows // 2)]),
                (bw.at[pl.ds(rows // 2, rows // 2)], wv.at[pl.ds(rows // 2, rows // 2)]),
                (row_ids, rowv),
                (col_ids, colv),
                (tv, tvv),
                (w3, w3v),
            ]
        )
    ]
    loads[0].start()
    loads[1].start()
    barrier = pltpu.get_barrier_semaphore()
    for d in far_first(CHIPS):
        signal(barrier, hub_peer(d), c)
    for d in range(1, NY):
        signal(barrier, y_dev(d, 1), c)
    signal(barrier, cross, c)
    for i in range(1, NZH):
        for d in range(1, NZL):
            signal(barrier, *z_dev(lax.rem(zh + i, NZH), zl(d)))
    for d in range(1, NZL):
        signal(barrier, b, zl(d) * NX + x)
    signal(barrier, b, z * NX + left)
    signal(barrier, b, z * NX + right)
    signal(barrier, sib, c)
    for k in loads[2:]:
        k.start()

    loads[0].wait()
    loads[1].wait()
    local_ids = idv[...] - b * rows
    lanes = jnp.concatenate([local_ids, local_ids], axis=1)
    step = 256
    picked = jnp.zeros((fl, TILE), F32)
    for i in range(rows // step):
        at = lax.broadcasted_iota(jnp.int32, (step, TILE), 0) + i * step
        hot = jnp.where(at == lanes, 1.0, 0.0).astype(BF)
        picked += jnp.dot(xe[:, TILE + i * step : TILE + (i + 1) * step], hot, preferred_element_type=F32)
    half = fl // 2
    low = lax.broadcasted_iota(jnp.int32, (half, TILE), 1) < TILE // 2
    hubs[0, chip] = jnp.where(low, picked[:half], picked[half:]).astype(BF)

    pl.semaphore_wait(barrier, CHIPS - 1 + NY - 1 + 1 + (NZH - 1) * (NZL - 1) + NZL - 1 + 2 + 1)

    def hub_copy(d):
        return rcopy(hubs.at[0, chip], hubs.at[0, chip], h_send.at[d], h_recv.at[d], hub_peer(d), c)

    for d in far_first(CHIPS):
        hub_copy(d).start()
    end = (blocks - 1) * TILE
    to_sib = rcopy(
        feat.at[:, pl.ds(pl.multiple_of((1 - core) * end, TILE), TILE)],
        xe.at[:, pl.ds(pl.multiple_of(core * (rows + TILE), TILE), TILE)],
        e_send.at[0], e_recv.at[0], sib, c,
    )
    to_cross = rcopy(
        feat.at[:, pl.ds(pl.multiple_of(core * end, TILE), TILE)],
        xe.at[:, pl.ds(pl.multiple_of((1 - core) * (rows + TILE), TILE), TILE)],
        e_send.at[1], e_recv.at[1], cross, c,
    )
    to_cross.start()
    to_sib.start()

    def part(ref, q):
        return ref.at[:, pl.ds(pl.multiple_of(q * quarter, TILE), quarter)]

    cots = [
        rcopy(part(cot, zl(d)), cotg.at[z], c_send.at[d - 1], c_recv.at[d - 1], b, zl(d) * NX + x)
        for d in range(1, NZL)
    ]
    own_cot = pltpu.make_async_copy(part(cot, z), cotg.at[z], c_loc)

    def do_band(r):
        band[r] = lax.dot_general(
            xe[:, r * TILE : (r + 3) * TILE], wv[r * TILE : (r + 1) * TILE, :], NT, preferred_element_type=F32
        )

    loads[2].wait()
    loads[3].wait()
    for r in range(1, blocks - 1):
        do_band(r)
    for k in loads[4:]:
        k.wait()
    same = lax.broadcasted_iota(jnp.int32, (blocks, slots), 0) == rowv[...] - b * blocks
    used = lax.broadcasted_iota(jnp.int32, (blocks, slots), 1) < count[0]
    place = jnp.where(same & used, 1.0, 0.0).astype(BF)
    place = jnp.concatenate([place, place], axis=1)

    for d in near_first(CHIPS):
        hub_copy(d).wait_recv()
    swap = rcopy(hubs.at[0], hubs.at[1], s_sem.at[0], s_sem.at[1], sib, c)
    swap.start()
    for k in cots:
        k.start()
    own_cot.start()
    to_cross.wait_recv()
    to_sib.wait_recv()
    do_band(0)
    do_band(blocks - 1)
    swap.wait_recv()

    mine = hubs[0].astype(F32)
    other = hubs[1].astype(F32)
    first = jnp.where(core == 0, mine, other)
    second = jnp.where(core == 0, other, mine)
    low3 = lax.broadcasted_iota(jnp.int32, mine.shape, 2) < TILE // 2
    hub[:, :half, :] = jnp.where(low3, first, pltpu.roll(second, TILE // 2, 2)).astype(BF)
    hub[:, half:, :] = jnp.where(low3, pltpu.roll(first, TILE // 2, 2), second).astype(BF)

    def some_pairs(i):
        for j in range(32):
            s = (i * 32 + j) * 2
            two = jnp.concatenate([hub[colv[s]], hub[colv[s + 1]]], axis=0)
            tiles = tvv[pl.ds(s, 2)].reshape(2 * TILE, TILE)
            got = lax.dot_general(two, tiles, NT, preferred_element_type=F32)
            part_s[pl.ds(s, fl, stride=slots), :] = got[:fl, :TILE]
            part_s[pl.ds(s + 1, fl, stride=slots), :] = got[fl:, TILE:]

    loop(0, slots // 64, some_pairs)
    for f in range(fl):
        value = part_s[f * slots : (f + 1) * slots, :]
        high = value.astype(BF)
        rest = (value - high.astype(F32)).astype(BF)
        hub_sum[pl.ds(f, blocks, stride=fl), :] = jnp.dot(
            place, jnp.concatenate([high, rest], axis=0), preferred_element_type=F32
        )

    wide = quarter // 2

    def side(ref, h):
        return ref.at[:, pl.ds(h * wide, wide)]

    def rounded(r):
        at = pl.ds(pl.multiple_of(r * fl, fl), fl)
        return (band[r] + hub_sum[at, :]).astype(BF)

    def z_copy(d, h):
        i = h * (NZL - 1) + d - 1
        return rcopy(side(aggq.at[zl(d)], h), side(g.at[c], h), z_send.at[i], z_recv.at[i], b, zl(d) * NX + x)

    def x_copy(src_z, src_x, h, to, way):
        slot = side(g.at[src_z * NX + src_x], h)
        return rcopy(slot, slot, x_send.at[way, h, src_z], x_recv.at[way, h, src_z], b, z * NX + to)

    def relay(src_z, h):
        origin, to = (left, right) if h == 0 else (right, left)
        slot = side(g.at[src_z * NX + origin], h)
        return rcopy(slot, slot, r_send.at[h, src_z], r_recv.at[h, src_z], b, z * NX + to)

    def source(d):
        return lax.rem(z + NZL - d, NZL)

    def push(d, h):
        x_copy(source(d), x, h, right, 0).start()
        x_copy(source(d), x, h, left, 1).start()

    def pass_on(d, h):
        x_copy(source(d), x, h, right, h).wait_recv()
        relay(source(d), h).start()

    turns = (1, 3, 2)
    for d in (2, 1, 3):
        for j in range(per):
            aggq[zl(d), :, j * TILE : (j + 1) * TILE] = rounded(zl(d) * per + j)
        z_copy(d, 0).start()
    for j in range(per):
        g[c, :, j * TILE : (j + 1) * TILE] = rounded(z * per + j)
    push(0, 0)
    for d in (2, 1, 3):
        z_copy(d, 1).start()
    push(0, 1)
    for n, d in enumerate(turns):
        z_copy(d, 0).wait_recv()
        push(d, 0)
        if n == 0:
            pass_on(0, 0)
        if n == 1:
            pass_on(0, 1)
    for d in turns:
        z_copy(d, 1).wait_recv()
        push(d, 1)
        pass_on(d, 0)
    for d in turns:
        pass_on(d, 1)
    for k in cots:
        k.wait_recv()
    own_cot.wait()

    feats = NZL * NX * fl
    mix = jnp.concatenate([w3v[s * NX + x] for s in range(NZL)], axis=0)

    def a_copy(d, h):
        i = h * (NZL - 1) + d - 1
        return rcopy(side(act.at[zl(d)], h), side(part(act_out, z), h), a_send.at[i], a_recv.at[i], b, zl(d) * NX + x)

    def own_act(h):
        return pltpu.make_async_copy(side(act.at[z], h), side(part(act_out, z), h), a_loc.at[h])

    halves = NZL * NX // NC

    def grad_part(k, h):
        cut = slice(h * wide, (h + 1) * wide)
        cols = g[pl.ds(k * halves, halves), :, cut].reshape(halves * fl, wide)
        return lax.dot_general(pres[:, cut], cols, NT, preferred_element_type=F32)

    step = 256
    for h in range(2):
        for d in range(NZL):
            x_copy(source(d), x, h, right, 1 - h).wait_recv()
            relay(source(d), h).wait_recv()
        for n in range(h * wide // step, (h + 1) * wide // step):
            cut = slice(n * step, (n + 1) * step)
            pre = jnp.dot(mix, g[:, :, cut].reshape(feats, step), preferred_element_type=F32)
            sig = jax.nn.sigmoid(pre)
            act[:, :, cut] = (pre * sig).astype(BF).reshape(NZL, fl, step)
            grad_in = cotg[:, :, cut].reshape(NZL * fl, step).astype(F32)
            pres[:, cut] = (grad_in * sig * (1.0 + pre * (1.0 - sig))).astype(BF)
        if h == 0:
            for d in range(1, NZL):
                a_copy(d, h).start()
            own_act(h).start()
            for k in range(NC):
                grads[k] = grad_part(k, h)


    def grad_half(k):
        got = grads[k] + grad_part(k, 1)
        for s in range(NZL):
            for j in range(NY):
                rt, lt = divmod(j, 2)
                pt[k, j, s] = got[s * fl + rt * 8 : s * fl + (rt + 1) * 8, lt * TILE : (lt + 1) * TILE]

    grad_half(1 - core)
    pair = rcopy(pt.at[1 - core], sb, p_sem.at[0], p_sem.at[1], sib, c)
    pair.start()
    for d in range(1, NZL):
        a_copy(d, 1).start()
    own_act(1).start()
    grad_half(core)
    pair.wait_recv()
    qb[...] = pt[core] + sb[...]

    def y_copy(d):
        return rcopy(qb.at[y_peer(d)], yb.at[d], y_send.at[d], y_recv.at[d], y_blk(y_peer(d)), c)

    for d in far_first(NY):
        y_copy(d).start()
    total = qb[y]
    for d in near_first(NY):
        y_copy(d).wait_recv()
        total = total + yb[d]
    st[...] = total

    def q_copy(d):
        return rcopy(st.at[z_peer(d)[1]], zb.at[d], q_send.at[d], q_recv.at[d], *z_dev(*z_peer(d)))

    for d in far_first(NZ):
        q_copy(d).start()
    tile = st[z]
    for d in near_first(NZ):
        q_copy(d).wait_recv()
        tile = tile + zb[d]
    wg_out[core, y] = tile

    def o_copy(d, k):
        spot = wg_out.at[core, y]
        return rcopy(spot, spot, o_send.at[k, d], o_recv.at[k, d], y_dev(d, k), c)

    for at in GRAD_STEPS:
        o_copy(*at).start()
    for at in GRAD_STEPS[::-1]:
        o_copy(*at).wait_recv()

    loop(1, CHIPS, lambda d: hub_copy(d).wait_send())
    swap.wait_send()
    to_cross.wait_send()
    to_sib.wait_send()
    for k in cots:
        k.wait_send()
    for h in range(2):
        for d in range(1, NZL):
            z_copy(d, h).wait_send()
        for d in range(NZL):
            x_copy(source(d), x, h, right, 0).wait_send()
            x_copy(source(d), x, h, left, 1).wait_send()
            relay(source(d), h).wait_send()
        for d in range(1, NZL):
            a_copy(d, h).wait_send()
            a_copy(d, h).wait_recv()
        own_act(h).wait()
    pair.wait_send()
    loop(1, NY, lambda d: y_copy(d).wait_send())
    loop(1, NZ, lambda d: q_copy(d).wait_send())
    for at in GRAD_STEPS:
        o_copy(*at).wait_send()


def write_kernel(act, tiles, act_out, grad_out, sem):
    copies = [pltpu.make_async_copy(act, act_out, sem.at[NC * NY])]
    for k in range(NC):
        for j in range(NY):
            rt, lt = divmod(j, 2)
            to = grad_out.at[pl.ds(rt * 8, 8), pl.ds((k * 2 + lt) * TILE, TILE)]
            copies.append(pltpu.make_async_copy(tiles.at[k, j], to, sem.at[k * NY + j]))
    for k in copies:
        k.start()
    for k in copies:
        k.wait()


DMA = pltpu.SemaphoreType.DMA


def body(
    features, band_weights, hub_ids, tile_rows, tile_cols, tile_vals, tile_counts, weight, cotangent
):
    fl, rows = features.shape
    blocks = rows // TILE
    quarter = rows // NZL
    slots = tile_vals.shape[0]
    cols = NZL * NX
    sds = jax.ShapeDtypeStruct
    act, wg = pl.pallas_call(
        layer_kernel,
        name="layer",
        out_shape=(sds((fl, rows), BF), sds((NC, NY, 8, TILE), F32)),
        in_specs=[SMEM] + [HBM] * 8,
        out_specs=(ANY, VMEM),
        scratch_shapes=[
            pltpu.VMEM((fl, rows + 2 * TILE), BF),
            pltpu.VMEM((rows, 3 * TILE), BF),
            pltpu.VMEM((1, hub_ids.shape[0]), jnp.int32),
            pltpu.VMEM((1, slots), jnp.int32),
            pltpu.SMEM((slots,), jnp.int32),
            pltpu.VMEM(tile_vals.shape, BF),
            pltpu.VMEM((NZL, fl, quarter), BF),
            pltpu.VMEM((cols, fl, weight.shape[1]), BF),
            pltpu.VMEM((blocks, fl, TILE), F32),
            pltpu.VMEM((2, CHIPS, fl // 2, TILE), BF),
            pltpu.VMEM((CHIPS, fl, TILE), BF),
            pltpu.VMEM((fl * slots, TILE), F32),
            pltpu.VMEM((blocks * fl, TILE), F32),
            pltpu.VMEM((NZL, fl, quarter), BF),
            pltpu.VMEM((cols, fl, quarter), BF),
            pltpu.VMEM((NZL, fl, quarter), BF),
            pltpu.VMEM((NZL * fl, quarter), BF),
            pltpu.VMEM((NC, NZL * fl, cols * fl // NC), F32),
            pltpu.VMEM((NC, NY, NZL, 8, TILE), F32),
            pltpu.VMEM((NY, NZL, 8, TILE), F32),
            pltpu.VMEM((NY, NZL, 8, TILE), F32),
            pltpu.VMEM((NY, NZL, 8, TILE), F32),
            pltpu.VMEM((NZL, 8, TILE), F32),
            pltpu.VMEM((NZ, 8, TILE), F32),
            DMA((8,)), DMA((CHIPS,)), DMA((CHIPS,)), DMA((2,)), DMA((2,)), DMA((2,)), DMA((3,)), DMA((3,)), DMA,
            DMA((6,)), DMA((6,)), DMA((2, 2, NZL)), DMA((2, 2, NZL)), DMA((2, NZL)), DMA((2, NZL)), DMA((6,)), DMA((6,)), DMA((2,)),
            DMA((2,)), DMA((NY,)), DMA((NY,)), DMA((NZ,)), DMA((NZ,)), DMA((NC, NY)), DMA((NC, NY)),
        ],
        compiler_params=pltpu.CompilerParams(
            collective_id=0, has_side_effects=True, vmem_limit_bytes=40 << 20
        ),
    )(
        tile_counts,
        *(
            pltpu.with_memory_space_constraint(k, pltpu.HBM)
            for k in (
                features, band_weights, hub_ids.reshape(1, -1), tile_rows.reshape(1, -1), tile_cols,
                tile_vals, cotangent, weight.reshape(cols, fl, weight.shape[1]),
            )
        ),
    )
    return pl.pallas_call(
        write_kernel,
        name="write",
        out_shape=(sds((fl, rows), BF), sds((fl, NC * NY * 8 * TILE // fl), F32)),
        in_specs=[VMEM, VMEM],
        out_specs=(HBM, HBM),
        scratch_shapes=[DMA((1 + NC * NY,))],
    )(pltpu.with_memory_space_constraint(act, pltpu.VMEM), pltpu.with_memory_space_constraint(wg, pltpu.VMEM))


def solution(mesh):
    in_specs = (
        P("col", "blk"),
        P("blk", None),
        P("blk"),
        P("blk"),
        P("blk"),
        P("blk", None, None),
        P("blk"),
        P(),
        P("col", "blk"),
    )
    out_specs = (P("col", "blk"), P("col", None))
    return jax.shard_map(body, mesh=mesh, in_specs=in_specs, out_specs=out_specs, check_vma=False)
```
